256 devices in a mesh: blk: 32 (over y_lo, z, core), band: 8 (over y_hi, x).
Axes of the slice: x: 4, y: 4 (y_hi: 2, y_lo: 2; y = y_hi * 2 + y_lo), z: 8, core: 2. Of those that a mesh axis runs over, the one named last changes fastest.
Arguments:
- spectra: bfloat16 [256, 3, 2, 320], P('blk', None, None, 'band'), may hold values from -6 to 6
- quality: int32 [256, 3], P('blk'), may hold values 0 or 1
Outputs:
- correlations: bfloat16 [32, 256, 8, 9, 128], P(None, 'blk', 'band')
The draws below stay inside these ranges and needn't reach their ends.
All inputs are finite; a program needn't handle non-finite values. No bound on the sum of `quality` on one device may be relied on, other than what follows from the above.
Results may differ from the reference program's by a relative error of at most 0.0012.
Values may be sent and summed in bfloat16 or wider, within the bound.
A program may use at most 64 MiB of HBM per device.

```python
import math
import jax
import jax.numpy as jnp
from jax import lax

F = 320
FIRST = 15
NFFT = 1500
MAXLAG = 64
LAGS = 128
TILE = 8
STATIONS = 256
N_BLK = 32


def with_ends(entries, stream_key, smallest, high):
    index_at = [jax.random.randint(jax.random.fold_in(stream_key, axis), (), 0, length) for axis, length in enumerate(entries.shape)]
    longest = entries.shape.index(max(entries.shape))
    next_to = index_at[:longest] + [(index_at[longest] + 1) % entries.shape[longest]] + index_at[longest + 1:]
    return entries.at[tuple(index_at)].set(smallest).at[tuple(next_to)].set(high)


def steps_of(stream_key, dims, split, least, largest):
    def one(dim, shards_of):
        draws = jax.random.uniform(jax.random.fold_in(jax.random.fold_in(stream_key, 6), dim), (shards_of,), jnp.float32, least / len(split), largest / len(split))
        return jnp.repeat(jnp.exp(draws), dims[dim] // shards_of).reshape((-1,) + (1,) * (len(dims) - dim - 1))

    gain = one(*split[0])
    for cut in split[1:]:
        gain = gain * one(*cut)
    return gain


def bell_draw(own_key, shape, spread, limit, split=(), kind=jnp.bfloat16):
    entries = jax.random.normal(own_key, shape, jnp.float32) * spread
    if len(split) > 0:
        entries = steps_of(own_key, shape, split, -0.22, 0.18) * entries
    return jnp.clip(entries, min=-limit, max=limit).astype(kind)


def setup_inputs(seed: int = 0) -> dict:
    key_list = jax.random.split(jax.random.key(seed), 3)
    return {
        "spectra": bell_draw(key_list[0], (STATIONS, 3, 2, F), 1.0, 6.0, ((0, 32), (3, 8))),
        "quality": with_ends((jax.random.randint(key_list[1], (STATIONS, 3), 0, 8) < 7).astype(jnp.int32), jax.random.fold_in(key_list[1], 1), 0, 1),
    }


def lag_transform():
    bins = jnp.arange(F, dtype=jnp.int32) + FIRST
    lag_steps = 2 * jnp.arange(LAGS, dtype=jnp.int32) - 2 * MAXLAG + 1
    phase_index = bins[:, None] * lag_steps[None, :] % (2 * NFFT)
    phases = math.pi / NFFT * phase_index.astype(jnp.float32)
    factor = 1.0 / math.sqrt(F)
    return jnp.stack([jnp.cos(phases) * factor, -jnp.sin(phases) * factor], axis=0)

def cross_spectra(left, right):
    left_count = left.shape[0]
    right_count = right.shape[0]
    bin_count = left.shape[3]
    left_real = left[:, :, 0, :][:, None, :, None, :]
    left_imag = left[:, :, 1, :][:, None, :, None, :]
    right_real = right[:, :, 0, :][None, :, None, :, :]
    right_imag = right[:, :, 1, :][None, :, None, :, :]
    real_part = left_real * right_real + left_imag * right_imag
    imag_part = left_imag * right_real - left_real * right_imag
    products = jnp.stack([real_part, imag_part], axis=4)
    return products.reshape(left_count * right_count * 9, 2 * bin_count)

def reference(spectra, quality):
    masked = (spectra * quality.astype(jnp.bfloat16)[:, :, None, None]).astype(jnp.float32)
    transform = lag_transform().reshape(2 * F, LAGS)
    tiles = masked.reshape(N_BLK, TILE, 3, 2, F)

    def row_tile(row_spectra):
        products = cross_spectra(row_spectra, masked)
        result = jnp.dot(products, transform, precision=lax.Precision.HIGHEST)
        return result.reshape(TILE, N_BLK, TILE, 9, LAGS).astype(jnp.bfloat16)
    stacked = lax.map(row_tile, tiles)
    return stacked.transpose(2, 0, 1, 3, 4, 5).reshape(N_BLK, STATIONS, TILE, 9, LAGS)
```

```python
import math

import jax
import jax.numpy as jnp
import numpy as np
from jax import lax
from jax.experimental import pallas as pl
from jax.experimental.pallas import tpu as pltpu
from jax.sharding import PartitionSpec as P

F = 320
FIRST = 15
NFFT = 1500
MAXLAG = 64
LAGS = 128
COMPS = 3
TILE = 8
N_BLK = 32
N_BAND = 8
BINS = F // N_BAND
HALF = 64
CHUNKS = F // HALF
DEPTH = 2 * F
LANES = 128
RING = 8
GROUP = 8
ROWS = GROUP * COMPS * COMPS * TILE
MESH = pl.DeviceIdType.MESH


def lag_table():
    bins = np.arange(F) + FIRST
    steps = 2 * np.arange(LAGS) - 2 * MAXLAG + 1
    index = bins[:, None] * steps[None, :] % (2 * NFFT)
    phase = (np.float32(math.pi / NFFT) * index.astype(np.float32)).astype(np.float64)
    factor = 1.0 / math.sqrt(F)
    both = np.stack([np.cos(phase) * factor, np.sin(phase) * factor])
    both = both.reshape(2, CHUNKS, HALF, LAGS).transpose(1, 0, 2, 3).reshape(DEPTH, LAGS)
    high = both.astype(jnp.bfloat16)
    low = (both - high.astype(np.float64)).astype(jnp.bfloat16)
    wide = np.concatenate([high, low], axis=1)
    return np.concatenate([wide, wide], axis=0)


def ring_offset(k):
    return (k + 1) // 2 if k % 2 else (RING - k // 2) % RING


def segments():
    found = []
    for p in range(N_BAND):
        at = 0
        while at < BINS:
            chunk, lane = divmod(p * BINS + at, HALF)
            length = min(BINS - at, HALF - lane)
            found.append((p, at, length, chunk, lane))
            at += length
    return found


def kernel(
    spec_hbm, qual_hbm, table_hbm, out_ref,
    spec_v, qual_v, table_v, pieces, tile_rows, left_same, left_cross, stations, wide_rows, products,
    load_sem, first_send, first_recv, second_send, second_recv,
):
    me = lax.axis_index("blk")
    band = lax.axis_index("band")
    my_y = me // (2 * RING)
    my_z = (me // 2) % RING
    my_core = me % 2

    def peer(k, other):
        flip_y, flip_core = divmod(other, 2)
        y = (my_y + flip_y) % 2
        z = (my_z + ring_offset(k)) % RING
        core = (my_core + flip_core) % 2
        return (y * RING + z) * 2 + core

    barrier = pltpu.get_barrier_semaphore()
    for step in range(1, N_BAND):
        pl.semaphore_signal(barrier, inc=1, device_id=(me, (band + step) % N_BAND), device_id_type=MESH)
    for step in range(1, N_BLK):
        pl.semaphore_signal(barrier, inc=1, device_id=((me + step) % N_BLK, band), device_id_type=MESH)
    loads = [
        pltpu.make_async_copy(spec_hbm, spec_v, load_sem.at[0]),
        pltpu.make_async_copy(qual_hbm, qual_v, load_sem.at[1]),
        pltpu.make_async_copy(table_hbm, table_v, load_sem.at[2]),
    ]
    for load in loads:
        load.start()
    loads[0].wait()
    loads[1].wait()

    quality = qual_v[...].astype(jnp.float32)
    row = lax.broadcasted_iota(jnp.int32, (TILE, TILE), 0)
    col = lax.broadcasted_iota(jnp.int32, (TILE, TILE), 1)
    raw = spec_v[...].astype(jnp.float32)
    parts = []
    for c in range(2):
        masked = []
        for a in range(COMPS):
            usable = jnp.sum(jnp.where(row == col, quality[a : a + 1, :], 0.0), axis=1, keepdims=True)
            masked.append(raw[:, a, c, :] * usable)
        masked.append(jnp.zeros((TILE, LANES - COMPS * BINS), jnp.float32))
        parts.append(jnp.concatenate(masked, axis=1))
    pieces[band] = jnp.concatenate(parts, axis=0).astype(jnp.bfloat16)

    pl.semaphore_wait(barrier, N_BAND + N_BLK - 2)

    def first(step):
        to = (band + step) % N_BAND
        return pltpu.make_async_remote_copy(
            src_ref=pieces.at[band], dst_ref=pieces.at[band],
            send_sem=first_send.at[to], recv_sem=first_recv.at[band],
            device_id=(me, to), device_id_type=MESH,
        )

    def first_arrival(step):
        at = (band + step) % N_BAND
        return pltpu.make_async_remote_copy(
            src_ref=pieces.at[at], dst_ref=pieces.at[at],
            send_sem=first_send.at[at], recv_sem=first_recv.at[at],
            device_id=(me, at), device_id_type=MESH,
        )

    for step in (6, 2, 5, 7, 3, 1, 4):
        first(step).start()
    for step in range(1, N_BAND):
        first_arrival(step).wait_recv()

    lane = lax.broadcasted_iota(jnp.int32, (TILE, LANES), 1)
    whole = [[None] * CHUNKS for _ in range(COMPS)]
    for p, at, length, chunk, start in segments():
        piece = pieces[p].astype(jnp.float32)
        for a in range(COMPS):
            for c in range(2):
                target = HALF * c + start
                moved = pltpu.roll(piece[TILE * c : TILE * (c + 1)], (target - BINS * a - at) % LANES, 1)
                if whole[a][chunk] is None:
                    whole[a][chunk] = moved
                else:
                    here = (lane >= target) & (lane < target + length)
                    whole[a][chunk] = jnp.where(here, moved, whole[a][chunk])
    for a in range(COMPS):
        for chunk in range(CHUNKS):
            tile_rows[pl.ds((a * CHUNKS + chunk) * TILE, TILE), :] = whole[a][chunk]
    tile_rows[pl.ds(COMPS * CHUNKS * TILE, TILE), :] = jnp.zeros((TILE, LANES), jnp.float32)
    stations[me] = tile_rows[pl.ds(band, 16, stride=TILE), :].astype(jnp.bfloat16)

    def second(k, other):
        to = peer(k, other)
        return pltpu.make_async_remote_copy(
            src_ref=stations.at[me], dst_ref=stations.at[me],
            send_sem=second_send.at[to], recv_sem=second_recv.at[me],
            device_id=(to, band), device_id_type=MESH,
        )

    def second_arrival(k, other):
        at = peer(k, other)
        return pltpu.make_async_remote_copy(
            src_ref=stations.at[at], dst_ref=stations.at[at],
            send_sem=second_send.at[at], recv_sem=second_recv.at[at],
            device_id=(at, band), device_id_type=MESH,
        )

    others = [(k, other) for k in range(RING) for other in range(4) if (k, other) != (0, 0)]
    for k, other in reversed(others):
        second(k, other).start()

    for a in range(COMPS):
        for chunk in range(CHUNKS):
            here = whole[a][chunk]
            turned = pltpu.roll(here, HALF, 1)
            left_same[a, chunk] = jnp.where(lane < HALF, here, turned)
            left_cross[a, chunk] = jnp.where(lane < HALF, turned, -here)
    loads[2].wait()

    for group in range(N_BLK // GROUP):
        members = [(2 * group + s // 4, s % 4) for s in range(GROUP)]
        for s, (k, other) in enumerate(members):
            if (k, other) != (0, 0):
                second_arrival(k, other).wait_recv()
            arrived = stations[peer(k, other)].astype(jnp.float32)
            wide_rows[s, 0] = arrived
            wide_rows[s, 1] = pltpu.roll(arrived, HALF, 1)
        for chunk in range(CHUNKS):
            for pair in range(GROUP // 2):
                for b in range(COMPS):
                    right = []
                    for s in (2 * pair, 2 * pair + 1):
                        at = b * CHUNKS + chunk
                        right.append((
                            jnp.broadcast_to(wide_rows[s, 0, at : at + 1, :], (TILE, LANES)),
                            jnp.broadcast_to(wide_rows[s, 1, at : at + 1, :], (TILE, LANES)),
                        ))
                    for a in range(COMPS):
                        same = left_same[a, chunk]
                        cross = left_cross[a, chunk]
                        value = jnp.concatenate([same * r + cross * t for r, t in right], axis=0)
                        high = value.astype(jnp.bfloat16)
                        low = (value - high.astype(jnp.float32)).astype(jnp.bfloat16)
                        where = pl.ds((pair * COMPS * COMPS + a * COMPS + b) * 2 * TILE, 2 * TILE)
                        products[where, chunk * LANES : (chunk + 1) * LANES] = high
                        products[where, DEPTH + chunk * LANES : DEPTH + (chunk + 1) * LANES] = low
        result = jnp.dot(products[...], table_v[...], preferred_element_type=jnp.float32)
        summed = (result[:, :LAGS] + result[:, LAGS:]).astype(jnp.bfloat16)
        for s, (k, other) in enumerate(members):
            at = peer(k, other)
            for ab in range(COMPS * COMPS):
                start = ((s // 2) * COMPS * COMPS + ab) * 2 * TILE + (s % 2) * TILE
                out_ref[at, ab] = summed[start : start + TILE]

    for step in range(1, N_BAND):
        first(step).wait_send()
    for k, other in others:
        second(k, other).wait_send()


def body(spectra, quality):
    out = pl.pallas_call(
        kernel,
        out_shape=jax.ShapeDtypeStruct((N_BLK, COMPS * COMPS, TILE, LAGS), jnp.bfloat16),
        in_specs=[pl.BlockSpec(memory_space=pl.ANY)] * 3,
        out_specs=pl.BlockSpec(memory_space=pltpu.VMEM),
        scratch_shapes=[
            pltpu.VMEM((TILE, COMPS, 2, BINS), jnp.bfloat16),
            pltpu.VMEM((COMPS, TILE), jnp.int32),
            pltpu.VMEM((2 * DEPTH, 2 * LAGS), jnp.bfloat16),
            pltpu.VMEM((N_BAND, 2 * TILE, LANES), jnp.bfloat16),
            pltpu.VMEM((16 * TILE, LANES), jnp.float32),
            pltpu.VMEM((COMPS, CHUNKS, TILE, LANES), jnp.float32),
            pltpu.VMEM((COMPS, CHUNKS, TILE, LANES), jnp.float32),
            pltpu.VMEM((N_BLK, 16, LANES), jnp.bfloat16),
            pltpu.VMEM((GROUP, 2, 16, LANES), jnp.float32),
            pltpu.VMEM((ROWS, 2 * DEPTH), jnp.bfloat16),
            pltpu.SemaphoreType.DMA((3,)),
            pltpu.SemaphoreType.DMA((N_BAND,)),
            pltpu.SemaphoreType.DMA((N_BAND,)),
            pltpu.SemaphoreType.DMA((N_BLK,)),
            pltpu.SemaphoreType.DMA((N_BLK,)),
        ],
        compiler_params=pltpu.CompilerParams(collective_id=0, has_side_effects=True),
    )(spectra, quality.T, jnp.asarray(lag_table()))
    return out.transpose(0, 2, 1, 3)[:, :, None]


def solution(mesh):
    placed = (P("blk", None, None, "band"), P("blk", None))
    return jax.shard_map(
        body,
        mesh=mesh,
        in_specs=placed,
        out_specs=P(None, "blk", "band", None, None),
        check_vma=False,
    )
```

```python
import math

import jax
import jax.numpy as jnp
import numpy as np
from jax import lax
from jax.experimental import pallas as pl
from jax.experimental.pallas import tpu as pltpu
from jax.sharding import PartitionSpec as P

F = 320
FIRST = 15
NFFT = 1500
MAXLAG = 64
LAGS = 128
COMPS = 3
TILE = 8
N_BLK = 32
N_BAND = 8
BINS = F // N_BAND
HALF = 64
CHUNKS = F // HALF
DEPTH = 2 * F
LANES = 128
RING = 8
GROUP = 8
ROWS = GROUP * COMPS * COMPS * TILE
MESH = pl.DeviceIdType.MESH


def lag_table():
    bins = np.arange(F) + FIRST
    steps = 2 * np.arange(LAGS) - 2 * MAXLAG + 1
    index = bins[:, None] * steps[None, :] % (2 * NFFT)
    phase = (np.float32(math.pi / NFFT) * index.astype(np.float32)).astype(np.float64)
    factor = 1.0 / math.sqrt(F)
    both = np.stack([np.cos(phase) * factor, np.sin(phase) * factor])
    both = both.reshape(2, CHUNKS, HALF, LAGS).transpose(1, 0, 2, 3).reshape(DEPTH, LAGS)
    high = both.astype(jnp.bfloat16)
    low = (both - high.astype(np.float64)).astype(jnp.bfloat16)
    wide = np.concatenate([high, low], axis=1)
    return np.concatenate([wide, wide], axis=0)


RING_ORDER = (0, 1, 2, 3, 7, 6, 5, 4)


def index_at(place):
    return ((place // 2) % 2 * RING + place // 4) * 2 + place % 2


def segments():
    found = []
    for p in range(N_BAND):
        at = 0
        while at < BINS:
            chunk, lane = divmod(p * BINS + at, HALF)
            length = min(BINS - at, HALF - lane)
            found.append((p, at, length, chunk, lane))
            at += length
    return found


def kernel(
    spec_hbm, qual_hbm, table_hbm, out_ref,
    spec_v, qual_v, table_v, pieces, tile_rows, left_same, left_cross, stations, wide_rows, products,
    entered, load_sem, first_send, first_recv, second_send, second_recv,
):
    me = lax.axis_index("blk")
    band = lax.axis_index("band")
    my_y = me // (2 * RING)
    my_z = (me // 2) % RING
    my_core = me % 2
    my_place = my_z * 4 + my_y * 2 + my_core

    def peer(k, other):
        flip_y, flip_core = divmod(other, 2)
        y = (my_y + flip_y) % 2
        z = (my_z + RING_ORDER[k]) % RING
        core = (my_core + flip_core) % 2
        return (y * RING + z) * 2 + core

    barrier = pltpu.get_barrier_semaphore()
    for step in range(1, N_BAND):
        pl.semaphore_signal(barrier, inc=1, device_id=(me, (band + step) % N_BAND), device_id_type=MESH)

    @pl.loop(my_place + 1, N_BLK)
    def _(place):
        pl.semaphore_signal(barrier, inc=1, device_id=(index_at(place), band), device_id_type=MESH)

    loads = [
        pltpu.make_async_copy(spec_hbm, spec_v, load_sem.at[0]),
        pltpu.make_async_copy(qual_hbm, qual_v, load_sem.at[1]),
        pltpu.make_async_copy(table_hbm, table_v, load_sem.at[2]),
    ]
    for load in loads:
        load.start()
    loads[0].wait()
    loads[1].wait()

    quality = qual_v[...].astype(jnp.float32)
    row = lax.broadcasted_iota(jnp.int32, (TILE, TILE), 0)
    col = lax.broadcasted_iota(jnp.int32, (TILE, TILE), 1)
    raw = spec_v[...].astype(jnp.float32)
    parts = []
    for c in range(2):
        masked = []
        for a in range(COMPS):
            usable = jnp.sum(jnp.where(row == col, quality[a : a + 1, :], 0.0), axis=1, keepdims=True)
            masked.append(raw[:, a, c, :] * usable)
        masked.append(jnp.zeros((TILE, LANES - COMPS * BINS), jnp.float32))
        parts.append(jnp.concatenate(masked, axis=1))
    pieces[band] = jnp.concatenate(parts, axis=0).astype(jnp.bfloat16)

    pl.semaphore_wait(barrier, N_BAND - 1 + my_place)

    def first(step):
        to = (band + step) % N_BAND
        return pltpu.make_async_remote_copy(
            src_ref=pieces.at[band], dst_ref=pieces.at[band],
            send_sem=first_send.at[to], recv_sem=first_recv.at[band],
            device_id=(me, to), device_id_type=MESH,
        )

    def first_arrival(step):
        at = (band + step) % N_BAND
        return pltpu.make_async_remote_copy(
            src_ref=pieces.at[at], dst_ref=pieces.at[at],
            send_sem=first_send.at[at], recv_sem=first_recv.at[at],
            device_id=(me, at), device_id_type=MESH,
        )

    for step in (6, 2, 5, 7, 3, 1, 4):
        first(step).start()

    @pl.loop(0, my_place)
    def _(place):
        pl.semaphore_signal(entered.at[me], inc=1, device_id=(index_at(place), band), device_id_type=MESH)

    for step in range(1, N_BAND):
        first_arrival(step).wait_recv()

    lane = lax.broadcasted_iota(jnp.int32, (TILE, LANES), 1)
    whole = [[None] * CHUNKS for _ in range(COMPS)]
    for p, at, length, chunk, start in segments():
        piece = pieces[p].astype(jnp.float32)
        for a in range(COMPS):
            for c in range(2):
                target = HALF * c + start
                moved = pltpu.roll(piece[TILE * c : TILE * (c + 1)], (target - BINS * a - at) % LANES, 1)
                if whole[a][chunk] is None:
                    whole[a][chunk] = moved
                else:
                    here = (lane >= target) & (lane < target + length)
                    whole[a][chunk] = jnp.where(here, moved, whole[a][chunk])
    for a in range(COMPS):
        for chunk in range(CHUNKS):
            tile_rows[pl.ds((a * CHUNKS + chunk) * TILE, TILE), :] = whole[a][chunk]
    tile_rows[pl.ds(COMPS * CHUNKS * TILE, TILE), :] = jnp.zeros((TILE, LANES), jnp.float32)
    stations[me] = tile_rows[pl.ds(band, 16, stride=TILE), :].astype(jnp.bfloat16)

    def second(at, to):
        return pltpu.make_async_remote_copy(
            src_ref=stations.at[at], dst_ref=stations.at[at],
            send_sem=second_send.at[to], recv_sem=second_recv.at[at],
            device_id=(to, band), device_id_type=MESH,
        )

    @pl.loop(0, my_place)
    def _(place):
        second(me, index_at(place)).start()

    @pl.loop(my_place + 1, N_BLK)
    def _(place):
        pl.semaphore_wait(entered.at[index_at(place)], 1)
        second(me, index_at(place)).start()

    for a in range(COMPS):
        for chunk in range(CHUNKS):
            here = whole[a][chunk]
            turned = pltpu.roll(here, HALF, 1)
            left_same[a, chunk] = jnp.where(lane < HALF, here, turned)
            left_cross[a, chunk] = jnp.where(lane < HALF, turned, -here)
    loads[2].wait()

    for group in range(N_BLK // GROUP):
        members = [(2 * group + s // 4, s % 4) for s in range(GROUP)]
        for s, (k, other) in enumerate(members):
            if (k, other) != (0, 0):
                second(peer(k, other), me).wait_recv()
            arrived = stations[peer(k, other)].astype(jnp.float32)
            wide_rows[s, 0] = arrived
            wide_rows[s, 1] = pltpu.roll(arrived, HALF, 1)
        for chunk in range(CHUNKS):
            for pair in range(GROUP // 2):
                for b in range(COMPS):
                    right = []
                    for s in (2 * pair, 2 * pair + 1):
                        at = b * CHUNKS + chunk
                        right.append((
                            jnp.broadcast_to(wide_rows[s, 0, at : at + 1, :], (TILE, LANES)),
                            jnp.broadcast_to(wide_rows[s, 1, at : at + 1, :], (TILE, LANES)),
                        ))
                    for a in range(COMPS):
                        same = left_same[a, chunk]
                        cross = left_cross[a, chunk]
                        value = jnp.concatenate([same * r + cross * t for r, t in right], axis=0)
                        high = value.astype(jnp.bfloat16)
                        low = (value - high.astype(jnp.float32)).astype(jnp.bfloat16)
                        where = pl.ds((pair * COMPS * COMPS + a * COMPS + b) * 2 * TILE, 2 * TILE)
                        products[where, chunk * LANES : (chunk + 1) * LANES] = high
                        products[where, DEPTH + chunk * LANES : DEPTH + (chunk + 1) * LANES] = low
        result = jnp.dot(products[...], table_v[...], preferred_element_type=jnp.float32)
        summed = (result[:, :LAGS] + result[:, LAGS:]).astype(jnp.bfloat16)
        for s, (k, other) in enumerate(members):
            at = peer(k, other)
            for ab in range(COMPS * COMPS):
                start = ((s // 2) * COMPS * COMPS + ab) * 2 * TILE + (s % 2) * TILE
                out_ref[at, ab] = summed[start : start + TILE]

    for step in range(1, N_BAND):
        first(step).wait_send()

    @pl.loop(1, N_BLK)
    def _(step):
        second(me, (me + step) % N_BLK).wait_send()


def body(spectra, quality):
    out = pl.pallas_call(
        kernel,
        out_shape=pltpu.VMEM((N_BLK, COMPS * COMPS, TILE, LAGS), jnp.bfloat16),
        in_specs=[pl.BlockSpec(memory_space=pl.ANY)] * 3,
        out_specs=pl.BlockSpec(memory_space=pltpu.VMEM),
        scratch_shapes=[
            pltpu.VMEM((TILE, COMPS, 2, BINS), jnp.bfloat16),
            pltpu.VMEM((COMPS, TILE), jnp.int32),
            pltpu.VMEM((2 * DEPTH, 2 * LAGS), jnp.bfloat16),
            pltpu.VMEM((N_BAND, 2 * TILE, LANES), jnp.bfloat16),
            pltpu.VMEM((16 * TILE, LANES), jnp.float32),
            pltpu.VMEM((COMPS, CHUNKS, TILE, LANES), jnp.float32),
            pltpu.VMEM((COMPS, CHUNKS, TILE, LANES), jnp.float32),
            pltpu.VMEM((N_BLK, 16, LANES), jnp.bfloat16),
            pltpu.VMEM((GROUP, 2, 16, LANES), jnp.float32),
            pltpu.VMEM((ROWS, 2 * DEPTH), jnp.bfloat16),
            pltpu.SemaphoreType.REGULAR((N_BLK,)),
            pltpu.SemaphoreType.DMA((3,)),
            pltpu.SemaphoreType.DMA((N_BAND,)),
            pltpu.SemaphoreType.DMA((N_BAND,)),
            pltpu.SemaphoreType.DMA((N_BLK,)),
            pltpu.SemaphoreType.DMA((N_BLK,)),
        ],
        compiler_params=pltpu.CompilerParams(collective_id=0, has_side_effects=True),
    )(spectra, quality.T, jnp.asarray(lag_table()))
    return out.transpose(0, 2, 1, 3)[:, :, None]


def solution(mesh):
    placed = (P("blk", None, None, "band"), P("blk", None))
    return jax.shard_map(
        body,
        mesh=mesh,
        in_specs=placed,
        out_specs=P(None, "blk", "band", None, None),
        check_vma=False,
    )
```

```python
import math

import jax
import jax.numpy as jnp
import numpy as np
from jax import lax
from jax.experimental import pallas as pl
from jax.experimental.pallas import tpu as pltpu
from jax.sharding import PartitionSpec as P

F = 320
FIRST = 15
NFFT = 1500
MAXLAG = 64
LAGS = 128
COMPS = 3
TILE = 8
N_BLK = 32
N_BAND = 8
BINS = F // N_BAND
HALF = 64
CHUNKS = F // HALF
DEPTH = 2 * F
LANES = 128
RING = 8
GROUP = 8
ROWS = GROUP * COMPS * COMPS * TILE
MESH = pl.DeviceIdType.MESH


def lag_table():
    bins = np.arange(F) + FIRST
    steps = 2 * np.arange(LAGS) - 2 * MAXLAG + 1
    index = bins[:, None] * steps[None, :] % (2 * NFFT)
    phase = (np.float32(math.pi / NFFT) * index.astype(np.float32)).astype(np.float64)
    factor = 1.0 / math.sqrt(F)
    both = np.stack([np.cos(phase) * factor, np.sin(phase) * factor])
    both = both.reshape(2, CHUNKS, HALF, LAGS).transpose(1, 0, 2, 3).reshape(DEPTH, LAGS)
    high = both.astype(jnp.bfloat16)
    low = (both - high.astype(np.float64)).astype(jnp.bfloat16)
    wide = np.concatenate([high, low], axis=1)
    return np.concatenate([wide, wide], axis=0)


RING_ORDER = (0, 1, 2, 3, 7, 6, 5, 4)
HUB = 30
HUB_ORDER = sorted((place for place in range(N_BLK) if place != HUB), key=lambda place: -min((place // 4 - HUB // 4) % RING, (HUB // 4 - place // 4) % RING))


def index_at(place):
    return ((place // 2) % 2 * RING + place // 4) * 2 + place % 2


def segments():
    found = []
    for p in range(N_BAND):
        at = 0
        while at < BINS:
            chunk, lane = divmod(p * BINS + at, HALF)
            length = min(BINS - at, HALF - lane)
            found.append((p, at, length, chunk, lane))
            at += length
    return found


def kernel(
    spec_hbm, qual_hbm, table_hbm, out_ref,
    spec_v, qual_v, table_v, pieces, tile_rows, left_same, left_cross, stations, wide_rows, products,
    all_in, load_sem, first_send, first_recv, second_send, second_recv,
):
    me = lax.axis_index("blk")
    band = lax.axis_index("band")
    my_y = lax.div(me, 2 * RING)
    my_z = lax.rem(lax.div(me, 2), RING)
    my_core = lax.rem(me, 2)
    my_place = my_z * 4 + my_y * 2 + my_core

    def peer(k, other):
        flip_y, flip_core = divmod(other, 2)
        y = lax.rem(my_y + flip_y, 2)
        z = lax.rem(my_z + RING_ORDER[k], RING)
        core = lax.rem(my_core + flip_core, 2)
        return (y * RING + z) * 2 + core

    loads = [
        pltpu.make_async_copy(spec_hbm, spec_v, load_sem.at[0]),
        pltpu.make_async_copy(qual_hbm, qual_v, load_sem.at[1]),
        pltpu.make_async_copy(table_hbm, table_v, load_sem.at[2]),
    ]
    for load in loads:
        load.start()

    barrier = pltpu.get_barrier_semaphore()

    @pl.when(my_place != HUB)
    def _():
        pl.semaphore_signal(barrier, inc=1, device_id=(index_at(HUB), band), device_id_type=MESH)

    for step in range(1, N_BAND):
        pl.semaphore_signal(barrier, inc=1, device_id=(me, lax.rem(band + step, N_BAND)), device_id_type=MESH)

    loads[0].wait()
    loads[1].wait()

    quality = qual_v[...].astype(jnp.float32)
    row = lax.broadcasted_iota(jnp.int32, (TILE, TILE), 0)
    col = lax.broadcasted_iota(jnp.int32, (TILE, TILE), 1)
    raw = spec_v[...].astype(jnp.float32)
    parts = []
    for c in range(2):
        masked = []
        for a in range(COMPS):
            usable = jnp.sum(jnp.where(row == col, quality[a : a + 1, :], 0.0), axis=1, keepdims=True)
            masked.append(raw[:, a, c, :] * usable)
        masked.append(jnp.zeros((TILE, LANES - COMPS * BINS), jnp.float32))
        parts.append(jnp.concatenate(masked, axis=1))
    pieces[band] = jnp.concatenate(parts, axis=0).astype(jnp.bfloat16)

    pl.semaphore_wait(barrier, jnp.where(my_place == HUB, N_BAND + N_BLK - 2, N_BAND - 1))

    @pl.when(my_place == HUB)
    def _():
        for place in HUB_ORDER:
            pl.semaphore_signal(all_in, inc=1, device_id=(index_at(place), band), device_id_type=MESH)

    def first(step):
        to = lax.rem(band + step, N_BAND)
        return pltpu.make_async_remote_copy(
            src_ref=pieces.at[band], dst_ref=pieces.at[band],
            send_sem=first_send, recv_sem=first_recv,
            device_id=(me, to), device_id_type=MESH,
        )

    for step in (6, 2, 5, 7, 3, 1, 4):
        first(step).start()

    all_first = pltpu.make_async_remote_copy(
        src_ref=pieces.at[pl.ds(0, N_BAND - 1)], dst_ref=pieces.at[pl.ds(0, N_BAND - 1)],
        send_sem=first_send, recv_sem=first_recv,
        device_id=(me, lax.rem(band + 1, N_BAND)), device_id_type=MESH,
    )
    all_first.wait_recv()

    lane = lax.broadcasted_iota(jnp.int32, (TILE, LANES), 1)
    whole = [[None] * CHUNKS for _ in range(COMPS)]
    for p, at, length, chunk, start in segments():
        piece = pieces[p].astype(jnp.float32)
        for a in range(COMPS):
            for c in range(2):
                target = HALF * c + start
                moved = pltpu.roll(piece[TILE * c : TILE * (c + 1)], (target - BINS * a - at) % LANES, 1)
                if whole[a][chunk] is None:
                    whole[a][chunk] = moved
                else:
                    here = (lane >= target) & (lane < target + length)
                    whole[a][chunk] = jnp.where(here, moved, whole[a][chunk])
    for a in range(COMPS):
        for chunk in range(CHUNKS):
            tile_rows[pl.ds((a * CHUNKS + chunk) * TILE, TILE), :] = whole[a][chunk]
    tile_rows[pl.ds(COMPS * CHUNKS * TILE, TILE), :] = jnp.zeros((TILE, LANES), jnp.float32)
    stations[me] = tile_rows[pl.ds(band, 16, stride=TILE), :].astype(jnp.bfloat16)

    def second(to):
        return pltpu.make_async_remote_copy(
            src_ref=stations.at[me], dst_ref=stations.at[me],
            send_sem=second_send, recv_sem=second_recv.at[my_z],
            device_id=(to, band), device_id_type=MESH,
        )

    def second_bytes(count, z):
        return pltpu.make_async_remote_copy(
            src_ref=stations.at[pl.ds(0, count)], dst_ref=stations.at[pl.ds(0, count)],
            send_sem=second_send, recv_sem=second_recv.at[z],
            device_id=(lax.rem(me + 1, N_BLK), band), device_id_type=MESH,
        )

    @pl.when(my_place != HUB)
    def _():
        pl.semaphore_wait(all_in, 1)

    for place in range(N_BLK):
        @pl.when(my_place != place)
        def _():
            second(index_at(place)).start()

    for a in range(COMPS):
        for chunk in range(CHUNKS):
            here = whole[a][chunk]
            turned = pltpu.roll(here, HALF, 1)
            left_same[a, chunk] = jnp.where(lane < HALF, here, turned)
            left_cross[a, chunk] = jnp.where(lane < HALF, turned, -here)
    loads[2].wait()

    for group in range(N_BLK // GROUP):
        members = [(2 * group + s // 4, s % 4) for s in range(GROUP)]
        for k in (2 * group, 2 * group + 1):
            second_bytes(4 if k else 3, lax.rem(my_z + RING_ORDER[k], RING)).wait_recv()
        for s, (k, other) in enumerate(members):
            arrived = stations[peer(k, other)].astype(jnp.float32)
            wide_rows[s, 0] = arrived
            wide_rows[s, 1] = pltpu.roll(arrived, HALF, 1)
        for chunk in range(CHUNKS):
            for pair in range(GROUP // 2):
                for b in range(COMPS):
                    right = []
                    for s in (2 * pair, 2 * pair + 1):
                        at = b * CHUNKS + chunk
                        right.append((
                            jnp.broadcast_to(wide_rows[s, 0, at : at + 1, :], (TILE, LANES)),
                            jnp.broadcast_to(wide_rows[s, 1, at : at + 1, :], (TILE, LANES)),
                        ))
                    for a in range(COMPS):
                        same = left_same[a, chunk]
                        cross = left_cross[a, chunk]
                        value = jnp.concatenate([same * r + cross * t for r, t in right], axis=0)
                        high = value.astype(jnp.bfloat16)
                        low = (value - high.astype(jnp.float32)).astype(jnp.bfloat16)
                        where = pl.ds((pair * COMPS * COMPS + a * COMPS + b) * 2 * TILE, 2 * TILE)
                        products[where, chunk * LANES : (chunk + 1) * LANES] = high
                        products[where, DEPTH + chunk * LANES : DEPTH + (chunk + 1) * LANES] = low
        result = jnp.dot(products[...], table_v[...], preferred_element_type=jnp.float32)
        summed = (result[:, :LAGS] + result[:, LAGS:]).astype(jnp.bfloat16)
        for s, (k, other) in enumerate(members):
            at = peer(k, other)
            for ab in range(COMPS * COMPS):
                start = ((s // 2) * COMPS * COMPS + ab) * 2 * TILE + (s % 2) * TILE
                out_ref[at, ab] = summed[start : start + TILE]

    all_first.wait_send()
    second_bytes(N_BLK - 1, my_z).wait_send()


def body(spectra, quality):
    out = pl.pallas_call(
        kernel,
        out_shape=pltpu.VMEM((N_BLK, COMPS * COMPS, TILE, LAGS), jnp.bfloat16),
        in_specs=[pl.BlockSpec(memory_space=pl.ANY)] * 3,
        out_specs=pl.BlockSpec(memory_space=pltpu.VMEM),
        scratch_shapes=[
            pltpu.VMEM((TILE, COMPS, 2, BINS), jnp.bfloat16),
            pltpu.VMEM((COMPS, TILE), jnp.int32),
            pltpu.VMEM((2 * DEPTH, 2 * LAGS), jnp.bfloat16),
            pltpu.VMEM((N_BAND, 2 * TILE, LANES), jnp.bfloat16),
            pltpu.VMEM((16 * TILE, LANES), jnp.float32),
            pltpu.VMEM((COMPS, CHUNKS, TILE, LANES), jnp.float32),
            pltpu.VMEM((COMPS, CHUNKS, TILE, LANES), jnp.float32),
            pltpu.VMEM((N_BLK, 16, LANES), jnp.bfloat16),
            pltpu.VMEM((GROUP, 2, 16, LANES), jnp.float32),
            pltpu.VMEM((ROWS, 2 * DEPTH), jnp.bfloat16),
            pltpu.SemaphoreType.REGULAR,
            pltpu.SemaphoreType.DMA((3,)),
            pltpu.SemaphoreType.DMA,
            pltpu.SemaphoreType.DMA,
            pltpu.SemaphoreType.DMA,
            pltpu.SemaphoreType.DMA((RING,)),
        ],
        compiler_params=pltpu.CompilerParams(collective_id=0, has_side_effects=True),
    )(spectra, quality.T, jnp.asarray(lag_table()))
    return out.transpose(0, 2, 1, 3)[:, :, None]


def solution(mesh):
    placed = (P("blk", None, None, "band"), P("blk", None))
    return jax.shard_map(
        body,
        mesh=mesh,
        in_specs=placed,
        out_specs=P(None, "blk", "band", None, None),
        check_vma=False,
    )
```

```python
import math

import jax
import jax.numpy as jnp
import numpy as np
from jax import lax
from jax.experimental import pallas as pl
from jax.experimental.pallas import tpu as pltpu
from jax.sharding import PartitionSpec as P

F = 320
FIRST = 15
NFFT = 1500
MAXLAG = 64
LAGS = 128
COMPS = 3
TILE = 8
N_BLK = 32
N_BAND = 8
BINS = F // N_BAND
HALF = 64
CHUNKS = F // HALF
DEPTH = 2 * F
LANES = 128
RING = 8
GROUP = 8
WIDE = 2 * LANES
STEPS = 3
UNITS = 2
MESH = pl.DeviceIdType.MESH


def lag_table():
    bins = np.arange(F) + FIRST
    steps = 2 * np.arange(LAGS) - 2 * MAXLAG + 1
    index = bins[:, None] * steps[None, :] % (2 * NFFT)
    phase = (np.float32(math.pi / NFFT) * index.astype(np.float32)).astype(np.float64)
    factor = 1.0 / math.sqrt(F)
    both = np.stack([np.cos(phase) * factor, np.sin(phase) * factor])
    both = both.reshape(2, CHUNKS, HALF, LAGS).transpose(1, 0, 2, 3).reshape(DEPTH, LAGS)
    high = both.astype(jnp.bfloat16)
    low = (both - high.astype(np.float64)).astype(jnp.bfloat16)
    wide = np.concatenate([high, low], axis=1)
    return np.concatenate([wide, wide[-LANES:]], axis=0)


RING_ORDER = (0, 1, 2, 3, 7, 6, 5, 4)
HUB = 30
HUB_ORDER = sorted((place for place in range(N_BLK) if place != HUB), key=lambda place: -min((place // 4 - HUB // 4) % RING, (HUB // 4 - place // 4) % RING))


def index_at(place):
    return ((place // 2) % 2 * RING + place // 4) * 2 + place % 2


def segments():
    found = []
    for p in range(N_BAND):
        at = 0
        while at < BINS:
            chunk, lane = divmod(p * BINS + at, HALF)
            length = min(BINS - at, HALF - lane)
            found.append((p, at, length, chunk, lane))
            at += length
    return found


def kernel(
    spec_hbm, qual_hbm, table_hbm, out_ref,
    spec_v, qual_v, table_v, pieces, tile_rows, left_same, left_cross, stations, wide_rows,
    all_in, load_sem, first_send, first_recv, second_send, second_recv,
):
    me = lax.axis_index("blk")
    band = lax.axis_index("band")
    my_y = lax.div(me, 2 * RING)
    my_z = lax.rem(lax.div(me, 2), RING)
    my_core = lax.rem(me, 2)
    my_place = my_z * 4 + my_y * 2 + my_core

    def peer(k, other):
        flip_y, flip_core = divmod(other, 2)
        y = lax.rem(my_y + flip_y, 2)
        z = lax.rem(my_z + RING_ORDER[k], RING)
        core = lax.rem(my_core + flip_core, 2)
        return (y * RING + z) * 2 + core

    loads = [
        pltpu.make_async_copy(spec_hbm, spec_v, load_sem.at[0]),
        pltpu.make_async_copy(qual_hbm, qual_v, load_sem.at[1]),
        pltpu.make_async_copy(table_hbm, table_v, load_sem.at[2]),
    ]
    for load in loads:
        load.start()

    barrier = pltpu.get_barrier_semaphore()

    @pl.when(my_place != HUB)
    def _():
        pl.semaphore_signal(barrier, inc=1, device_id=(index_at(HUB), band), device_id_type=MESH)

    for step in range(1, N_BAND):
        pl.semaphore_signal(barrier, inc=1, device_id=(me, lax.rem(band + step, N_BAND)), device_id_type=MESH)

    loads[0].wait()
    loads[1].wait()

    quality = qual_v[...].astype(jnp.float32)
    row = lax.broadcasted_iota(jnp.int32, (TILE, TILE), 0)
    col = lax.broadcasted_iota(jnp.int32, (TILE, TILE), 1)
    raw = spec_v[...].astype(jnp.float32)
    parts = []
    for c in range(2):
        masked = []
        for a in range(COMPS):
            usable = jnp.sum(jnp.where(row == col, quality[a : a + 1, :], 0.0), axis=1, keepdims=True)
            masked.append(raw[:, a, c, :] * usable)
        masked.append(jnp.zeros((TILE, LANES - COMPS * BINS), jnp.float32))
        parts.append(jnp.concatenate(masked, axis=1))
    pieces[band] = jnp.concatenate(parts, axis=0).astype(jnp.bfloat16)

    pl.semaphore_wait(barrier, jnp.where(my_place == HUB, N_BAND + N_BLK - 2, N_BAND - 1))

    @pl.when(my_place == HUB)
    def _():
        for place in HUB_ORDER:
            pl.semaphore_signal(all_in, inc=1, device_id=(index_at(place), band), device_id_type=MESH)

    def first(step):
        to = lax.rem(band + step, N_BAND)
        return pltpu.make_async_remote_copy(
            src_ref=pieces.at[band], dst_ref=pieces.at[band],
            send_sem=first_send, recv_sem=first_recv,
            device_id=(me, to), device_id_type=MESH,
        )

    for step in (6, 2, 5, 7, 3, 1, 4):
        first(step).start()

    all_first = pltpu.make_async_remote_copy(
        src_ref=pieces.at[pl.ds(0, N_BAND - 1)], dst_ref=pieces.at[pl.ds(0, N_BAND - 1)],
        send_sem=first_send, recv_sem=first_recv,
        device_id=(me, lax.rem(band + 1, N_BAND)), device_id_type=MESH,
    )
    all_first.wait_recv()

    lane = lax.broadcasted_iota(jnp.int32, (TILE, LANES), 1)
    whole = [[None] * CHUNKS for _ in range(COMPS)]
    for p, at, length, chunk, start in segments():
        piece = pieces[p].astype(jnp.float32)
        for a in range(COMPS):
            for c in range(2):
                target = HALF * c + start
                moved = pltpu.roll(piece[TILE * c : TILE * (c + 1)], (target - BINS * a - at) % LANES, 1)
                if whole[a][chunk] is None:
                    whole[a][chunk] = moved
                else:
                    here = (lane >= target) & (lane < target + length)
                    whole[a][chunk] = jnp.where(here, moved, whole[a][chunk])
    for a in range(COMPS):
        for chunk in range(CHUNKS):
            tile_rows[pl.ds((a * CHUNKS + chunk) * TILE, TILE), :] = whole[a][chunk]
    tile_rows[pl.ds(COMPS * CHUNKS * TILE, TILE), :] = jnp.zeros((TILE, LANES), jnp.float32)
    stations[me] = tile_rows[pl.ds(band, 16, stride=TILE), :].astype(jnp.bfloat16)

    def second(to):
        return pltpu.make_async_remote_copy(
            src_ref=stations.at[me], dst_ref=stations.at[me],
            send_sem=second_send, recv_sem=second_recv.at[my_z],
            device_id=(to, band), device_id_type=MESH,
        )

    def second_bytes(count, z):
        return pltpu.make_async_remote_copy(
            src_ref=stations.at[pl.ds(0, count)], dst_ref=stations.at[pl.ds(0, count)],
            send_sem=second_send, recv_sem=second_recv.at[z],
            device_id=(lax.rem(me + 1, N_BLK), band), device_id_type=MESH,
        )

    @pl.when(my_place != HUB)
    def _():
        pl.semaphore_wait(all_in, 1)

    for place in range(N_BLK):
        @pl.when(my_place != place)
        def _():
            second(index_at(place)).start()

    for a in range(COMPS):
        for chunk in range(CHUNKS):
            here = whole[a][chunk]
            turned = pltpu.roll(here, HALF, 1)
            left_same[a, chunk] = jnp.where(lane < HALF, here, turned)
            left_cross[a, chunk] = jnp.where(lane < HALF, turned, -here)
    loads[2].wait()

    def split_cross(pair, a, b, chunk):
        rows = []
        at = b * CHUNKS + chunk
        for s in (2 * pair, 2 * pair + 1):
            straight = jnp.broadcast_to(wide_rows[s, 0, at : at + 1, :], (TILE, LANES))
            turned = jnp.broadcast_to(wide_rows[s, 1, at : at + 1, :], (TILE, LANES))
            rows.append(left_same[a, chunk] * straight + left_cross[a, chunk] * turned)
        value = jnp.concatenate(rows, axis=0)
        high = value.astype(jnp.bfloat16)
        return high, (value - high.astype(jnp.float32)).astype(jnp.bfloat16)

    def correlate(*totals):
        for group in range(N_BLK // GROUP):
            members = [(2 * group + s // 4, s % 4) for s in range(GROUP)]
            for k in (2 * group, 2 * group + 1):
                second_bytes(4 if k else 3, lax.rem(my_z + RING_ORDER[k], RING)).wait_recv()
            for s, (k, other) in enumerate(members):
                arrived = stations[peer(k, other)].astype(jnp.float32)
                wide_rows[s, 0] = arrived
                wide_rows[s, 1] = pltpu.roll(arrived, HALF, 1)
            for step in range(STEPS):
                register = (group * STEPS + step) % 2
                weights = table_v[pl.ds(step * WIDE, WIDE), :]
                for unit in range(UNITS):
                    pltpu.matmul_push_rhs(weights, staging_register=register, mxu_index=unit)
                fresh = [True] * UNITS
                for pair in range(GROUP // 2):
                    unit = pair % UNITS
                    for b in range(COMPS):
                        for a in range(COMPS):
                            parts = [split_cross(pair, a, b, chunk) for chunk in range(2 * step, min(2 * step + 2, CHUNKS))]
                            sums = totals[pair * COMPS * COMPS + a * COMPS + b]
                            if len(parts) == 1:
                                operands = [jnp.concatenate(parts[0], axis=1)]
                            else:
                                operands = [jnp.concatenate([part[i] for part in parts], axis=1) for i in range(2)]
                            for operand in operands:
                                pltpu.matmul_acc_lhs(sums, operand, load_staged_rhs=register if fresh[unit] else None)
                                fresh[unit] = False
            for pair in range(GROUP // 2):
                for ab in range(COMPS * COMPS):
                    both = pltpu.matmul_pop(totals[pair * COMPS * COMPS + ab])
                    summed = both[:, :LAGS] + both[:, LAGS:]
                    for half in range(2):
                        k, other = members[2 * pair + half]
                        out_ref[peer(k, other), ab] = summed[half * TILE : (half + 1) * TILE].astype(jnp.bfloat16)

    pl.run_scoped(
        correlate,
        *[pltpu.ACC(i // (COMPS * COMPS) % UNITS)((2 * TILE, WIDE), jnp.float32) for i in range(GROUP // 2 * COMPS * COMPS)],
    )
    all_first.wait_send()
    second_bytes(N_BLK - 1, my_z).wait_send()


def body(spectra, quality):
    out = pl.pallas_call(
        kernel,
        out_shape=pltpu.VMEM((N_BLK, COMPS * COMPS, TILE, LAGS), jnp.bfloat16),
        in_specs=[pl.BlockSpec(memory_space=pl.ANY)] * 3,
        out_specs=pl.BlockSpec(memory_space=pltpu.VMEM),
        scratch_shapes=[
            pltpu.VMEM((TILE, COMPS, 2, BINS), jnp.bfloat16),
            pltpu.VMEM((COMPS, TILE), jnp.int32),
            pltpu.VMEM((DEPTH + LANES, 2 * LAGS), jnp.bfloat16),
            pltpu.VMEM((N_BAND, 2 * TILE, LANES), jnp.bfloat16),
            pltpu.VMEM((16 * TILE, LANES), jnp.float32),
            pltpu.VMEM((COMPS, CHUNKS, TILE, LANES), jnp.float32),
            pltpu.VMEM((COMPS, CHUNKS, TILE, LANES), jnp.float32),
            pltpu.VMEM((N_BLK, 16, LANES), jnp.bfloat16),
            pltpu.VMEM((GROUP, 2, 16, LANES), jnp.float32),
            pltpu.SemaphoreType.REGULAR,
            pltpu.SemaphoreType.DMA((3,)),
            pltpu.SemaphoreType.DMA,
            pltpu.SemaphoreType.DMA,
            pltpu.SemaphoreType.DMA,
            pltpu.SemaphoreType.DMA((RING,)),
        ],
        compiler_params=pltpu.CompilerParams(collective_id=0, has_side_effects=True),
    )(spectra, quality.T, jnp.asarray(lag_table()))
    return out.transpose(0, 2, 1, 3)[:, :, None]


def solution(mesh):
    placed = (P("blk", None, None, "band"), P("blk", None))
    return jax.shard_map(
        body,
        mesh=mesh,
        in_specs=placed,
        out_specs=P(None, "blk", "band", None, None),
        check_vma=False,
    )
```

```python
import math

import jax
import jax.numpy as jnp
import numpy as np
from jax import lax
from jax.experimental import pallas as pl
from jax.experimental.pallas import tpu as pltpu
from jax.sharding import PartitionSpec as P

F = 320
FIRST = 15
NFFT = 1500
MAXLAG = 64
LAGS = 128
COMPS = 3
TILE = 8
N_BLK = 32
N_BAND = 8
BINS = F // N_BAND
HALF = 64
CHUNKS = F // HALF
DEPTH = 2 * F
LANES = 128
RING = 8
GROUP = 8
WIDE = 2 * LANES
STEPS = 3
UNITS = 2
MESH = pl.DeviceIdType.MESH


def lag_table():
    bins = np.arange(F) + FIRST
    steps = 2 * np.arange(LAGS) - 2 * MAXLAG + 1
    index = bins[:, None] * steps[None, :] % (2 * NFFT)
    phase = (np.float32(math.pi / NFFT) * index.astype(np.float32)).astype(np.float64)
    factor = 1.0 / math.sqrt(F)
    both = np.stack([np.cos(phase) * factor, np.sin(phase) * factor])
    both = both.reshape(2, CHUNKS, HALF, LAGS).transpose(1, 0, 2, 3).reshape(DEPTH, LAGS)
    high = both.astype(jnp.bfloat16)
    low = (both - high.astype(np.float64)).astype(jnp.bfloat16)
    wide = np.concatenate([high, low], axis=1)
    return np.concatenate([wide, wide[-LANES:]], axis=0)


RING_ORDER = (0, 1, 2, 3, 7, 6, 5, 4)
HUB_Z = (3, 5, 6, 6, 6, 7, 7, 7)
HUB_ORDER = [4 * z + other for z in (4, 3, 5, 2, 6, 1, 7, 0) for other in range(4)]


def index_at(place):
    return ((place // 2) % 2 * RING + place // 4) * 2 + place % 2


def segments():
    found = []
    for p in range(N_BAND):
        at = 0
        while at < BINS:
            chunk, lane = divmod(p * BINS + at, HALF)
            length = min(BINS - at, HALF - lane)
            found.append((p, at, length, chunk, lane))
            at += length
    return found


def kernel(
    spec_hbm, qual_hbm, table_hbm, out_ref,
    spec_v, qual_v, table_v, pieces, rows_out, rows_in, left_same, left_cross, stations, wide_rows,
    all_in, load_sem, first_send, first_recv, second_send, second_recv, third_send, third_recv,
):
    me = lax.axis_index("blk")
    band = lax.axis_index("band")
    my_y = lax.div(me, 2 * RING)
    my_z = lax.rem(lax.div(me, 2), RING)
    my_core = lax.rem(me, 2)
    my_place = my_z * 4 + my_y * 2 + my_core

    def peer(k, other):
        flip_y, flip_core = divmod(other, 2)
        y = lax.rem(my_y + flip_y, 2)
        z = lax.rem(my_z + RING_ORDER[k], RING)
        core = lax.rem(my_core + flip_core, 2)
        return (y * RING + z) * 2 + core

    loads = [
        pltpu.make_async_copy(spec_hbm, spec_v, load_sem.at[0]),
        pltpu.make_async_copy(qual_hbm, qual_v, load_sem.at[1]),
        pltpu.make_async_copy(table_hbm, table_v, load_sem.at[2]),
    ]
    for load in loads:
        load.start()

    hub_z = HUB_Z[-1]
    for b in range(N_BAND - 1):
        hub_z = jnp.where(band == b, HUB_Z[b], hub_z)
    hub = 4 * hub_z + 2
    barrier = pltpu.get_barrier_semaphore()

    @pl.when(my_place != hub)
    def _():
        pl.semaphore_signal(barrier, inc=1, device_id=(index_at(hub), band), device_id_type=MESH)

    for step in range(1, N_BAND):
        pl.semaphore_signal(barrier, inc=1, device_id=(me, lax.rem(band + step, N_BAND)), device_id_type=MESH)

    loads[0].wait()
    loads[1].wait()

    quality = qual_v[...].astype(jnp.float32)
    row = lax.broadcasted_iota(jnp.int32, (TILE, TILE), 0)
    col = lax.broadcasted_iota(jnp.int32, (TILE, TILE), 1)
    raw = spec_v[...].astype(jnp.float32)
    parts = []
    for c in range(2):
        masked = []
        for a in range(COMPS):
            usable = jnp.sum(jnp.where(row == col, quality[a : a + 1, :], 0.0), axis=1, keepdims=True)
            masked.append(raw[:, a, c, :] * usable)
        masked.append(jnp.zeros((TILE, LANES - COMPS * BINS), jnp.float32))
        parts.append(jnp.concatenate(masked, axis=1))
    pieces[band] = jnp.concatenate(parts, axis=0).astype(jnp.bfloat16)
    flat = jnp.concatenate(parts, axis=1)
    for station in range(TILE):
        rows_out[station] = flat[station : station + 1, :]
    rows_in[band] = rows_out[band]

    pl.semaphore_wait(barrier, jnp.where(my_place == hub, N_BAND + N_BLK - 2, N_BAND - 1))

    @pl.when(my_place == hub)
    def _():
        for place in HUB_ORDER:
            @pl.when(my_place != place)
            def _():
                pl.semaphore_signal(all_in, inc=1, device_id=(index_at(place), band), device_id_type=MESH)

    def first(step):
        to = lax.rem(band + step, N_BAND)
        return pltpu.make_async_remote_copy(
            src_ref=rows_out.at[to], dst_ref=rows_in.at[band],
            send_sem=first_send, recv_sem=first_recv,
            device_id=(me, to), device_id_type=MESH,
        )

    def third(step):
        to = lax.rem(band + step, N_BAND)
        return pltpu.make_async_remote_copy(
            src_ref=pieces.at[band], dst_ref=pieces.at[band],
            send_sem=third_send, recv_sem=third_recv,
            device_id=(me, to), device_id_type=MESH,
        )

    def whole_bytes(ref, send_sem, recv_sem):
        return pltpu.make_async_remote_copy(
            src_ref=ref.at[pl.ds(0, N_BAND - 1)], dst_ref=ref.at[pl.ds(0, N_BAND - 1)],
            send_sem=send_sem, recv_sem=recv_sem,
            device_id=(me, lax.rem(band + 1, N_BAND)), device_id_type=MESH,
        )

    for step in (6, 2, 5, 7, 3, 1, 4):
        first(step).start()
    all_first = whole_bytes(rows_in, first_send, first_recv)
    all_third = whole_bytes(pieces, third_send, third_recv)

    lane = lax.broadcasted_iota(jnp.int32, (TILE, LANES), 1)

    def assemble(piece):
        whole = [[None] * CHUNKS for _ in range(COMPS)]
        for p, at, length, chunk, start in segments():
            for c in range(2):
                values = piece(p, c)
                for a in range(COMPS):
                    target = HALF * c + start
                    moved = pltpu.roll(values, (target - BINS * a - at) % LANES, 1)
                    if whole[a][chunk] is None:
                        whole[a][chunk] = moved
                    else:
                        here = (lane >= target) & (lane < target + length)
                        whole[a][chunk] = jnp.where(here, moved, whole[a][chunk])
        return whole

    all_first.wait_recv()
    mine = assemble(lambda p, c: jnp.broadcast_to(rows_in[p, :, c * LANES : (c + 1) * LANES], (TILE, LANES)))
    sublane = lax.broadcasted_iota(jnp.int32, (TILE, LANES), 0)
    halves = []
    for half in range(2):
        rows = jnp.zeros((TILE, LANES), jnp.float32)
        for r in range(TILE):
            if half * TILE + r < COMPS * CHUNKS:
                a, chunk = divmod(half * TILE + r, CHUNKS)
                rows = jnp.where(sublane == r, mine[a][chunk], rows)
        halves.append(rows)
    stations[me] = jnp.concatenate(halves, axis=0).astype(jnp.bfloat16)

    def second(to):
        return pltpu.make_async_remote_copy(
            src_ref=stations.at[me], dst_ref=stations.at[me],
            send_sem=second_send, recv_sem=second_recv.at[my_z],
            device_id=(to, band), device_id_type=MESH,
        )

    def second_bytes(count, z):
        return pltpu.make_async_remote_copy(
            src_ref=stations.at[pl.ds(0, count)], dst_ref=stations.at[pl.ds(0, count)],
            send_sem=second_send, recv_sem=second_recv.at[z],
            device_id=(lax.rem(me + 1, N_BLK), band), device_id_type=MESH,
        )

    @pl.when(my_place != hub)
    def _():
        pl.semaphore_wait(all_in, 1)

    for place in range(N_BLK):
        @pl.when(my_place != place)
        def _():
            second(index_at(place)).start()

    for step in (6, 2, 5, 7, 3, 1, 4):
        third(step).start()
    all_third.wait_recv()
    whole = assemble(lambda p, c: pieces[p, c * TILE : (c + 1) * TILE, :].astype(jnp.float32))

    for a in range(COMPS):
        for chunk in range(CHUNKS):
            here = whole[a][chunk]
            turned = pltpu.roll(here, HALF, 1)
            left_same[a, chunk] = jnp.where(lane < HALF, here, turned)
            left_cross[a, chunk] = jnp.where(lane < HALF, turned, -here)
    loads[2].wait()

    def split_cross(pair, a, b, chunk):
        rows = []
        at = b * CHUNKS + chunk
        for s in (2 * pair, 2 * pair + 1):
            straight = jnp.broadcast_to(wide_rows[s, 0, at : at + 1, :], (TILE, LANES))
            turned = jnp.broadcast_to(wide_rows[s, 1, at : at + 1, :], (TILE, LANES))
            rows.append(left_same[a, chunk] * straight + left_cross[a, chunk] * turned)
        value = jnp.concatenate(rows, axis=0)
        high = value.astype(jnp.bfloat16)
        return high, (value - high.astype(jnp.float32)).astype(jnp.bfloat16)

    def correlate(*totals):
        for group in range(N_BLK // GROUP):
            members = [divmod(group * GROUP + s, 4) for s in range(GROUP)]
            for k in sorted({k for k, _ in members}):
                second_bytes(4 if k else 3, lax.rem(my_z + RING_ORDER[k], RING)).wait_recv()
            for s, (k, other) in enumerate(members):
                arrived = stations[peer(k, other)].astype(jnp.float32)
                wide_rows[s, 0] = arrived
                wide_rows[s, 1] = pltpu.roll(arrived, HALF, 1)
            for step in range(STEPS):
                register = (group * STEPS + step) % 2
                weights = table_v[pl.ds(step * WIDE, WIDE), :]
                for unit in range(UNITS):
                    pltpu.matmul_push_rhs(weights, staging_register=register, mxu_index=unit)
                fresh = [True] * UNITS
                for pair in range(GROUP // 2):
                    unit = pair % UNITS
                    for b in range(COMPS):
                        for a in range(COMPS):
                            parts = [split_cross(pair, a, b, chunk) for chunk in range(2 * step, min(2 * step + 2, CHUNKS))]
                            sums = totals[pair * COMPS * COMPS + a * COMPS + b]
                            if len(parts) == 1:
                                operands = [jnp.concatenate(parts[0], axis=1)]
                            else:
                                operands = [jnp.concatenate([part[i] for part in parts], axis=1) for i in range(2)]
                            for operand in operands:
                                pltpu.matmul_acc_lhs(sums, operand, load_staged_rhs=register if fresh[unit] else None)
                                fresh[unit] = False
            for pair in range(GROUP // 2):
                for ab in range(COMPS * COMPS):
                    both = pltpu.matmul_pop(totals[pair * COMPS * COMPS + ab])
                    summed = both[:, :LAGS] + both[:, LAGS:]
                    for half in range(2):
                        k, other = members[2 * pair + half]
                        out_ref[peer(k, other), ab] = summed[half * TILE : (half + 1) * TILE].astype(jnp.bfloat16)

    pl.run_scoped(
        correlate,
        *[pltpu.ACC(i // (COMPS * COMPS) % UNITS)((2 * TILE, WIDE), jnp.float32) for i in range(GROUP // 2 * COMPS * COMPS)],
    )
    all_first.wait_send()
    all_third.wait_send()
    second_bytes(N_BLK - 1, my_z).wait_send()


def body(spectra, quality):
    out = pl.pallas_call(
        kernel,
        out_shape=pltpu.VMEM((N_BLK, COMPS * COMPS, TILE, LAGS), jnp.bfloat16),
        in_specs=[pl.BlockSpec(memory_space=pl.ANY)] * 3,
        out_specs=pl.BlockSpec(memory_space=pltpu.VMEM),
        scratch_shapes=[
            pltpu.VMEM((TILE, COMPS, 2, BINS), jnp.bfloat16),
            pltpu.VMEM((COMPS, TILE), jnp.int32),
            pltpu.VMEM((DEPTH + LANES, 2 * LAGS), jnp.bfloat16),
            pltpu.VMEM((N_BAND, 2 * TILE, LANES), jnp.bfloat16),
            pltpu.VMEM((N_BAND, 1, 2 * LANES), jnp.float32),
            pltpu.VMEM((N_BAND, 1, 2 * LANES), jnp.float32),
            pltpu.VMEM((COMPS, CHUNKS, TILE, LANES), jnp.float32),
            pltpu.VMEM((COMPS, CHUNKS, TILE, LANES), jnp.float32),
            pltpu.VMEM((N_BLK, 16, LANES), jnp.bfloat16),
            pltpu.VMEM((GROUP, 2, 16, LANES), jnp.float32),
            pltpu.SemaphoreType.REGULAR,
            pltpu.SemaphoreType.DMA((3,)),
            pltpu.SemaphoreType.DMA,
            pltpu.SemaphoreType.DMA,
            pltpu.SemaphoreType.DMA,
            pltpu.SemaphoreType.DMA((RING,)),
            pltpu.SemaphoreType.DMA,
            pltpu.SemaphoreType.DMA,
        ],
        compiler_params=pltpu.CompilerParams(collective_id=0, has_side_effects=True),
    )(spectra, quality.T, jnp.asarray(lag_table()))
    return out.transpose(0, 2, 1, 3)[:, :, None]


def solution(mesh):
    placed = (P("blk", None, None, "band"), P("blk", None))
    return jax.shard_map(
        body,
        mesh=mesh,
        in_specs=placed,
        out_specs=P(None, "blk", "band", None, None),
        check_vma=False,
    )
```

```python
import math

import jax
import jax.numpy as jnp
import numpy as np
from jax import lax
from jax.experimental import pallas as pl
from jax.experimental.pallas import tpu as pltpu
from jax.sharding import PartitionSpec as P

F = 320
FIRST = 15
NFFT = 1500
MAXLAG = 64
LAGS = 128
COMPS = 3
TILE = 8
N_BLK = 32
N_BAND = 8
BINS = F // N_BAND
HALF = 64
CHUNKS = F // HALF
DEPTH = 2 * F
LANES = 128
RING = 8
GROUP = 8
WIDE = 2 * LANES
STEPS = 3
UNITS = 2
MESH = pl.DeviceIdType.MESH


def lag_table():
    bins = np.arange(F) + FIRST
    steps = 2 * np.arange(LAGS) - 2 * MAXLAG + 1
    index = bins[:, None] * steps[None, :] % (2 * NFFT)
    phase = (np.float32(math.pi / NFFT) * index.astype(np.float32)).astype(np.float64)
    factor = 1.0 / math.sqrt(F)
    both = np.stack([np.cos(phase) * factor, np.sin(phase) * factor])
    both = both.reshape(2, CHUNKS, HALF, LAGS).transpose(1, 0, 2, 3).reshape(DEPTH, LAGS)
    high = both.astype(jnp.bfloat16)
    low = (both - high.astype(np.float64)).astype(jnp.bfloat16)
    wide = np.concatenate([high, low], axis=1)
    return np.concatenate([wide, wide[-LANES:]], axis=0)


RING_ORDER = (0, 1, 2, 3, 7, 6, 5, 4)
HUB_Z = (3, 5, 6, 6, 6, 7, 7, 7)
HUB_ORDER = [4 * z + other for z in (4, 3, 5, 2, 6, 1, 7, 0) for other in range(4)]


def index_at(place):
    return ((place // 2) % 2 * RING + place // 4) * 2 + place % 2


def segments():
    found = []
    for p in range(N_BAND):
        at = 0
        while at < BINS:
            chunk, lane = divmod(p * BINS + at, HALF)
            length = min(BINS - at, HALF - lane)
            found.append((p, at, length, chunk, lane))
            at += length
    return found


def kernel(
    spec_hbm, qual_hbm, table_hbm, out_ref,
    spec_v, qual_v, table_v, pieces, rows_out, rows_in, left_same, left_cross, stations, wide_rows,
    all_in, load_sem, first_send, first_recv, second_send, second_recv, third_send, third_recv,
):
    me = lax.axis_index("blk")
    band = lax.axis_index("band")
    my_y = lax.div(me, 2 * RING)
    my_z = lax.rem(lax.div(me, 2), RING)
    my_core = lax.rem(me, 2)
    my_place = my_z * 4 + my_y * 2 + my_core

    def peer(k, other):
        flip_y, flip_core = divmod(other, 2)
        y = lax.rem(my_y + flip_y, 2)
        z = lax.rem(my_z + RING_ORDER[k], RING)
        core = lax.rem(my_core + flip_core, 2)
        return (y * RING + z) * 2 + core

    loads = [
        pltpu.make_async_copy(spec_hbm, spec_v, load_sem.at[0]),
        pltpu.make_async_copy(qual_hbm, qual_v, load_sem.at[1]),
        pltpu.make_async_copy(table_hbm, table_v, load_sem.at[2]),
    ]
    for load in loads:
        load.start()

    hub_z = HUB_Z[-1]
    for b in range(N_BAND - 1):
        hub_z = jnp.where(band == b, HUB_Z[b], hub_z)
    hub = 4 * hub_z + 2
    barrier = pltpu.get_barrier_semaphore()

    @pl.when(my_place != hub)
    def _():
        pl.semaphore_signal(barrier, inc=1, device_id=(index_at(hub), band), device_id_type=MESH)

    for step in range(1, N_BAND):
        pl.semaphore_signal(barrier, inc=1, device_id=(me, lax.rem(band + step, N_BAND)), device_id_type=MESH)

    loads[0].wait()
    loads[1].wait()

    quality = qual_v[...].astype(jnp.float32)
    row = lax.broadcasted_iota(jnp.int32, (TILE, TILE), 0)
    col = lax.broadcasted_iota(jnp.int32, (TILE, TILE), 1)
    raw = spec_v[...].astype(jnp.float32)
    parts = []
    for c in range(2):
        masked = []
        for a in range(COMPS):
            usable = jnp.sum(jnp.where(row == col, quality[a : a + 1, :], 0.0), axis=1, keepdims=True)
            masked.append(raw[:, a, c, :] * usable)
        masked.append(jnp.zeros((TILE, LANES - COMPS * BINS), jnp.float32))
        parts.append(jnp.concatenate(masked, axis=1))
    pieces[band] = jnp.concatenate(parts, axis=0).astype(jnp.bfloat16)
    flat = jnp.concatenate(parts, axis=1)
    for station in range(TILE):
        rows_out[station] = flat[station : station + 1, :]
    rows_in[band] = rows_out[band]

    pl.semaphore_wait(barrier, jnp.where(my_place == hub, N_BAND + N_BLK - 2, N_BAND - 1))

    @pl.when(my_place == hub)
    def _():
        for place in HUB_ORDER:
            @pl.when(my_place != place)
            def _():
                pl.semaphore_signal(all_in, inc=1, device_id=(index_at(place), band), device_id_type=MESH)

    def first(step):
        to = lax.rem(band + step, N_BAND)
        return pltpu.make_async_remote_copy(
            src_ref=rows_out.at[to], dst_ref=rows_in.at[band],
            send_sem=first_send, recv_sem=first_recv,
            device_id=(me, to), device_id_type=MESH,
        )

    def third(step):
        to = lax.rem(band + step, N_BAND)
        return pltpu.make_async_remote_copy(
            src_ref=pieces.at[band], dst_ref=pieces.at[band],
            send_sem=third_send, recv_sem=third_recv,
            device_id=(me, to), device_id_type=MESH,
        )

    def whole_bytes(ref, send_sem, recv_sem):
        return pltpu.make_async_remote_copy(
            src_ref=ref.at[pl.ds(0, N_BAND - 1)], dst_ref=ref.at[pl.ds(0, N_BAND - 1)],
            send_sem=send_sem, recv_sem=recv_sem,
            device_id=(me, lax.rem(band + 1, N_BAND)), device_id_type=MESH,
        )

    for step in (6, 2, 5, 7, 3, 1, 4):
        first(step).start()
    for step in (6, 2, 5, 7, 3, 1, 4):
        third(step).start()
    all_first = whole_bytes(rows_in, first_send, first_recv)
    all_third = whole_bytes(pieces, third_send, third_recv)

    lane = lax.broadcasted_iota(jnp.int32, (TILE, LANES), 1)

    def assemble(piece):
        whole = [[None] * CHUNKS for _ in range(COMPS)]
        for p, at, length, chunk, start in segments():
            for c in range(2):
                values = piece(p, c)
                for a in range(COMPS):
                    target = HALF * c + start
                    moved = pltpu.roll(values, (target - BINS * a - at) % LANES, 1)
                    if whole[a][chunk] is None:
                        whole[a][chunk] = moved
                    else:
                        here = (lane >= target) & (lane < target + length)
                        whole[a][chunk] = jnp.where(here, moved, whole[a][chunk])
        return whole

    all_first.wait_recv()
    mine = assemble(lambda p, c: jnp.broadcast_to(rows_in[p, :, c * LANES : (c + 1) * LANES], (TILE, LANES)))
    sublane = lax.broadcasted_iota(jnp.int32, (TILE, LANES), 0)
    halves = []
    for half in range(2):
        rows = jnp.zeros((TILE, LANES), jnp.float32)
        for r in range(TILE):
            if half * TILE + r < COMPS * CHUNKS:
                a, chunk = divmod(half * TILE + r, CHUNKS)
                rows = jnp.where(sublane == r, mine[a][chunk], rows)
        halves.append(rows)
    stations[me] = jnp.concatenate(halves, axis=0).astype(jnp.bfloat16)

    def second(to):
        return pltpu.make_async_remote_copy(
            src_ref=stations.at[me], dst_ref=stations.at[me],
            send_sem=second_send, recv_sem=second_recv.at[my_z],
            device_id=(to, band), device_id_type=MESH,
        )

    def second_bytes(count, z):
        return pltpu.make_async_remote_copy(
            src_ref=stations.at[pl.ds(0, count)], dst_ref=stations.at[pl.ds(0, count)],
            send_sem=second_send, recv_sem=second_recv.at[z],
            device_id=(lax.rem(me + 1, N_BLK), band), device_id_type=MESH,
        )

    @pl.when(my_place != hub)
    def _():
        pl.semaphore_wait(all_in, 1)

    for place in [1, 3, 0, 2] + list(range(4, N_BLK)):
        @pl.when(my_place != place)
        def _():
            second(index_at(place)).start()

    all_third.wait_recv()
    whole = assemble(lambda p, c: pieces[p, c * TILE : (c + 1) * TILE, :].astype(jnp.float32))

    for a in range(COMPS):
        for chunk in range(CHUNKS):
            here = whole[a][chunk]
            turned = pltpu.roll(here, HALF, 1)
            left_same[a, chunk] = jnp.where(lane < HALF, here, turned)
            left_cross[a, chunk] = jnp.where(lane < HALF, turned, -here)
    loads[2].wait()

    def split_cross(pair, a, b, chunk):
        rows = []
        at = b * CHUNKS + chunk
        for s in (2 * pair, 2 * pair + 1):
            straight = jnp.broadcast_to(wide_rows[s, 0, at : at + 1, :], (TILE, LANES))
            turned = jnp.broadcast_to(wide_rows[s, 1, at : at + 1, :], (TILE, LANES))
            rows.append(left_same[a, chunk] * straight + left_cross[a, chunk] * turned)
        value = jnp.concatenate(rows, axis=0)
        high = value.astype(jnp.bfloat16)
        return high, (value - high.astype(jnp.float32)).astype(jnp.bfloat16)

    def correlate(*totals):
        for group in range(N_BLK // GROUP):
            members = [divmod(group * GROUP + s, 4) for s in range(GROUP)]
            for k in sorted({k for k, _ in members}):
                second_bytes(4 if k else 3, lax.rem(my_z + RING_ORDER[k], RING)).wait_recv()
            for s, (k, other) in enumerate(members):
                arrived = stations[peer(k, other)].astype(jnp.float32)
                wide_rows[s, 0] = arrived
                wide_rows[s, 1] = pltpu.roll(arrived, HALF, 1)
            for step in range(STEPS):
                register = (group * STEPS + step) % 2
                weights = table_v[pl.ds(step * WIDE, WIDE), :]
                for unit in range(UNITS):
                    pltpu.matmul_push_rhs(weights, staging_register=register, mxu_index=unit)
                fresh = [True] * UNITS
                for pair in range(GROUP // 2):
                    unit = pair % UNITS
                    for b in range(COMPS):
                        for a in range(COMPS):
                            parts = [split_cross(pair, a, b, chunk) for chunk in range(2 * step, min(2 * step + 2, CHUNKS))]
                            sums = totals[pair * COMPS * COMPS + a * COMPS + b]
                            if len(parts) == 1:
                                operands = [jnp.concatenate(parts[0], axis=1)]
                            else:
                                operands = [jnp.concatenate([part[i] for part in parts], axis=1) for i in range(2)]
                            for operand in operands:
                                pltpu.matmul_acc_lhs(sums, operand, load_staged_rhs=register if fresh[unit] else None)
                                fresh[unit] = False
            for pair in range(GROUP // 2):
                for ab in range(COMPS * COMPS):
                    both = pltpu.matmul_pop(totals[pair * COMPS * COMPS + ab])
                    summed = both[:, :LAGS] + both[:, LAGS:]
                    for half in range(2):
                        k, other = members[2 * pair + half]
                        out_ref[peer(k, other), ab] = summed[half * TILE : (half + 1) * TILE].astype(jnp.bfloat16)

    pl.run_scoped(
        correlate,
        *[pltpu.ACC(i // (COMPS * COMPS) % UNITS)((2 * TILE, WIDE), jnp.float32) for i in range(GROUP // 2 * COMPS * COMPS)],
    )
    all_first.wait_send()
    all_third.wait_send()
    second_bytes(N_BLK - 1, my_z).wait_send()


def body(spectra, quality):
    out = pl.pallas_call(
        kernel,
        out_shape=pltpu.VMEM((N_BLK, COMPS * COMPS, TILE, LAGS), jnp.bfloat16),
        in_specs=[pl.BlockSpec(memory_space=pl.ANY)] * 3,
        out_specs=pl.BlockSpec(memory_space=pltpu.VMEM),
        scratch_shapes=[
            pltpu.VMEM((TILE, COMPS, 2, BINS), jnp.bfloat16),
            pltpu.VMEM((COMPS, TILE), jnp.int32),
            pltpu.VMEM((DEPTH + LANES, 2 * LAGS), jnp.bfloat16),
            pltpu.VMEM((N_BAND, 2 * TILE, LANES), jnp.bfloat16),
            pltpu.VMEM((N_BAND, 1, 2 * LANES), jnp.float32),
            pltpu.VMEM((N_BAND, 1, 2 * LANES), jnp.float32),
            pltpu.VMEM((COMPS, CHUNKS, TILE, LANES), jnp.float32),
            pltpu.VMEM((COMPS, CHUNKS, TILE, LANES), jnp.float32),
            pltpu.VMEM((N_BLK, 16, LANES), jnp.bfloat16),
            pltpu.VMEM((GROUP, 2, 16, LANES), jnp.float32),
            pltpu.SemaphoreType.REGULAR,
            pltpu.SemaphoreType.DMA((3,)),
            pltpu.SemaphoreType.DMA,
            pltpu.SemaphoreType.DMA,
            pltpu.SemaphoreType.DMA,
            pltpu.SemaphoreType.DMA((RING,)),
            pltpu.SemaphoreType.DMA,
            pltpu.SemaphoreType.DMA,
        ],
        compiler_params=pltpu.CompilerParams(collective_id=0, has_side_effects=True),
    )(spectra, quality.T, jnp.asarray(lag_table()))
    return out.transpose(0, 2, 1, 3)[:, :, None]


def solution(mesh):
    placed = (P("blk", None, None, "band"), P("blk", None))
    return jax.shard_map(
        body,
        mesh=mesh,
        in_specs=placed,
        out_specs=P(None, "blk", "band", None, None),
        check_vma=False,
    )
```

```python
import math

import jax
import jax.numpy as jnp
import numpy as np
from jax import lax
from jax.experimental import pallas as pl
from jax.experimental.pallas import tpu as pltpu
from jax.sharding import PartitionSpec as P

F = 320
FIRST = 15
NFFT = 1500
MAXLAG = 64
LAGS = 128
COMPS = 3
TILE = 8
N_BLK = 32
N_BAND = 8
BINS = F // N_BAND
HALF = 64
CHUNKS = F // HALF
DEPTH = 2 * F
LANES = 128
RING = 8
GROUP = 8
WIDE = 2 * LANES
STEPS = 3
UNITS = 2
MESH = pl.DeviceIdType.MESH


def lag_table():
    bins = np.arange(F) + FIRST
    steps = 2 * np.arange(LAGS) - 2 * MAXLAG + 1
    index = bins[:, None] * steps[None, :] % (2 * NFFT)
    phase = (np.float32(math.pi / NFFT) * index.astype(np.float32)).astype(np.float64)
    factor = 1.0 / math.sqrt(F)
    both = np.stack([np.cos(phase) * factor, np.sin(phase) * factor])
    both = both.reshape(2, CHUNKS, HALF, LAGS).transpose(1, 0, 2, 3).reshape(DEPTH, LAGS)
    high = both.astype(jnp.bfloat16)
    low = (both - high.astype(np.float64)).astype(jnp.bfloat16)
    wide = np.concatenate([high, low], axis=1)
    return np.concatenate([wide, wide[-LANES:]], axis=0)


RING_ORDER = (0, 1, 2, 3, 7, 6, 5, 4)
HUB_Z = (3, 5, 6, 6, 6, 7, 7, 7)
HUB_ORDER = [4 * z + other for z in (4, 3, 5, 2, 6, 1, 7, 0) for other in range(4)]


def index_at(place):
    return ((place // 2) % 2 * RING + place // 4) * 2 + place % 2


def segments():
    found = []
    for p in range(N_BAND):
        at = 0
        while at < BINS:
            chunk, lane = divmod(p * BINS + at, HALF)
            length = min(BINS - at, HALF - lane)
            found.append((p, at, length, chunk, lane))
            at += length
    return found


def kernel(
    spec_hbm, qual_hbm, table_hbm, out_ref,
    spec_v, qual_v, table_v, pieces, rows_out, rows_in, left_same, left_cross, stations, wide_rows,
    all_in, load_sem, first_send, first_recv, second_send, second_recv, third_send, third_recv,
):
    me = lax.axis_index("blk")
    band = lax.axis_index("band")
    my_y = lax.div(me, 2 * RING)
    my_z = lax.rem(lax.div(me, 2), RING)
    my_core = lax.rem(me, 2)
    my_place = my_z * 4 + my_y * 2 + my_core

    def peer(k, other):
        flip_y, flip_core = divmod(other, 2)
        y = lax.rem(my_y + flip_y, 2)
        z = lax.rem(my_z + RING_ORDER[k], RING)
        core = lax.rem(my_core + flip_core, 2)
        return (y * RING + z) * 2 + core

    loads = [
        pltpu.make_async_copy(spec_hbm, spec_v, load_sem.at[0]),
        pltpu.make_async_copy(qual_hbm, qual_v, load_sem.at[1]),
        pltpu.make_async_copy(table_hbm, table_v, load_sem.at[2]),
    ]
    loads[0].start()
    loads[1].start()

    hub_z = HUB_Z[-1]
    for b in range(N_BAND - 1):
        hub_z = jnp.where(band == b, HUB_Z[b], hub_z)
    hub = 4 * hub_z + 2
    barrier = pltpu.get_barrier_semaphore()

    @pl.when(my_place != hub)
    def _():
        pl.semaphore_signal(barrier, inc=1, device_id=(index_at(hub), band), device_id_type=MESH)

    for step in (6, 2, 5, 7, 3, 1, 4):
        pl.semaphore_signal(barrier, inc=1, device_id=(me, lax.rem(band + step, N_BAND)), device_id_type=MESH)

    loads[0].wait()
    loads[1].wait()

    quality = qual_v[...].astype(jnp.float32)
    row = lax.broadcasted_iota(jnp.int32, (TILE, TILE), 0)
    col = lax.broadcasted_iota(jnp.int32, (TILE, TILE), 1)
    raw = spec_v[...].astype(jnp.float32)
    parts = []
    for c in range(2):
        masked = []
        for a in range(COMPS):
            usable = jnp.sum(jnp.where(row == col, quality[a : a + 1, :], 0.0), axis=1, keepdims=True)
            masked.append(raw[:, a, c, :] * usable)
        masked.append(jnp.zeros((TILE, LANES - COMPS * BINS), jnp.float32))
        parts.append(jnp.concatenate(masked, axis=1))
    pieces[band] = jnp.concatenate(parts, axis=0).astype(jnp.bfloat16)
    flat = jnp.concatenate(parts, axis=1)
    for station in range(TILE):
        rows_out[station] = flat[station : station + 1, :]
    rows_in[band] = rows_out[band]

    pl.semaphore_wait(barrier, jnp.where(my_place == hub, N_BAND + N_BLK - 2, N_BAND - 1))

    @pl.when(my_place == hub)
    def _():
        for place in HUB_ORDER:
            @pl.when(my_place != place)
            def _():
                pl.semaphore_signal(all_in, inc=1, device_id=(index_at(place), band), device_id_type=MESH)

    def first(step):
        to = lax.rem(band + step, N_BAND)
        return pltpu.make_async_remote_copy(
            src_ref=rows_out.at[to], dst_ref=rows_in.at[band],
            send_sem=first_send, recv_sem=first_recv,
            device_id=(me, to), device_id_type=MESH,
        )

    def third(step):
        to = lax.rem(band + step, N_BAND)
        return pltpu.make_async_remote_copy(
            src_ref=pieces.at[band], dst_ref=pieces.at[band],
            send_sem=third_send, recv_sem=third_recv,
            device_id=(me, to), device_id_type=MESH,
        )

    def whole_bytes(ref, send_sem, recv_sem):
        return pltpu.make_async_remote_copy(
            src_ref=ref.at[pl.ds(0, N_BAND - 1)], dst_ref=ref.at[pl.ds(0, N_BAND - 1)],
            send_sem=send_sem, recv_sem=recv_sem,
            device_id=(me, lax.rem(band + 1, N_BAND)), device_id_type=MESH,
        )

    for step in (6, 2, 5, 7, 3, 1, 4):
        first(step).start()
    for step in (6, 2, 5, 7, 3, 1, 4):
        third(step).start()
    loads[2].start()
    all_first = whole_bytes(rows_in, first_send, first_recv)
    all_third = whole_bytes(pieces, third_send, third_recv)

    lane = lax.broadcasted_iota(jnp.int32, (TILE, LANES), 1)

    def assemble(piece):
        whole = [[None] * CHUNKS for _ in range(COMPS)]
        for p, at, length, chunk, start in segments():
            for c in range(2):
                values = piece(p, c)
                for a in range(COMPS):
                    target = HALF * c + start
                    moved = pltpu.roll(values, (target - BINS * a - at) % LANES, 1)
                    if whole[a][chunk] is None:
                        whole[a][chunk] = moved
                    else:
                        here = (lane >= target) & (lane < target + length)
                        whole[a][chunk] = jnp.where(here, moved, whole[a][chunk])
        return whole

    all_first.wait_recv()
    mine = assemble(lambda p, c: jnp.broadcast_to(rows_in[p, :, c * LANES : (c + 1) * LANES], (TILE, LANES)))
    sublane = lax.broadcasted_iota(jnp.int32, (TILE, LANES), 0)
    halves = []
    for half in range(2):
        rows = jnp.zeros((TILE, LANES), jnp.float32)
        for r in range(TILE):
            if half * TILE + r < COMPS * CHUNKS:
                a, chunk = divmod(half * TILE + r, CHUNKS)
                rows = jnp.where(sublane == r, mine[a][chunk], rows)
        halves.append(rows)
    stations[me] = jnp.concatenate(halves, axis=0).astype(jnp.bfloat16)

    def second(to):
        return pltpu.make_async_remote_copy(
            src_ref=stations.at[me], dst_ref=stations.at[me],
            send_sem=second_send, recv_sem=second_recv.at[my_z],
            device_id=(to, band), device_id_type=MESH,
        )

    def second_bytes(count, z):
        return pltpu.make_async_remote_copy(
            src_ref=stations.at[pl.ds(0, count)], dst_ref=stations.at[pl.ds(0, count)],
            send_sem=second_send, recv_sem=second_recv.at[z],
            device_id=(lax.rem(me + 1, N_BLK), band), device_id_type=MESH,
        )

    @pl.when(my_place != hub)
    def _():
        pl.semaphore_wait(all_in, 1)

    for place in [1, 3, 0, 2] + list(range(4, N_BLK)):
        @pl.when(my_place != place)
        def _():
            second(index_at(place)).start()

    all_third.wait_recv()
    whole = assemble(lambda p, c: pieces[p, c * TILE : (c + 1) * TILE, :].astype(jnp.float32))

    for a in range(COMPS):
        for chunk in range(CHUNKS):
            here = whole[a][chunk]
            turned = pltpu.roll(here, HALF, 1)
            left_same[a, chunk] = jnp.where(lane < HALF, here, turned)
            left_cross[a, chunk] = jnp.where(lane < HALF, turned, -here)
    loads[2].wait()

    def split_cross(pair, a, b, chunk):
        rows = []
        at = b * CHUNKS + chunk
        for s in (2 * pair, 2 * pair + 1):
            straight = jnp.broadcast_to(wide_rows[s, 0, at : at + 1, :], (TILE, LANES))
            turned = jnp.broadcast_to(wide_rows[s, 1, at : at + 1, :], (TILE, LANES))
            rows.append(left_same[a, chunk] * straight + left_cross[a, chunk] * turned)
        value = jnp.concatenate(rows, axis=0)
        high = value.astype(jnp.bfloat16)
        return high, (value - high.astype(jnp.float32)).astype(jnp.bfloat16)

    def correlate(*totals):
        for group in range(N_BLK // GROUP):
            members = [divmod(group * GROUP + s, 4) for s in range(GROUP)]
            for k in sorted({k for k, _ in members}):
                second_bytes(4 if k else 3, lax.rem(my_z + RING_ORDER[k], RING)).wait_recv()
            for s, (k, other) in enumerate(members):
                arrived = stations[peer(k, other)].astype(jnp.float32)
                wide_rows[s, 0] = arrived
                wide_rows[s, 1] = pltpu.roll(arrived, HALF, 1)
            for step in range(STEPS):
                register = (group * STEPS + step) % 2
                weights = table_v[pl.ds(step * WIDE, WIDE), :]
                for unit in range(UNITS):
                    pltpu.matmul_push_rhs(weights, staging_register=register, mxu_index=unit)
                fresh = [True] * UNITS
                for pair in range(GROUP // 2):
                    unit = pair % UNITS
                    for b in range(COMPS):
                        for a in range(COMPS):
                            parts = [split_cross(pair, a, b, chunk) for chunk in range(2 * step, min(2 * step + 2, CHUNKS))]
                            sums = totals[pair * COMPS * COMPS + a * COMPS + b]
                            if len(parts) == 1:
                                operands = [jnp.concatenate(parts[0], axis=1)]
                            else:
                                operands = [jnp.concatenate([part[i] for part in parts], axis=1) for i in range(2)]
                            for operand in operands:
                                pltpu.matmul_acc_lhs(sums, operand, load_staged_rhs=register if fresh[unit] else None)
                                fresh[unit] = False
            for pair in range(GROUP // 2):
                for ab in range(COMPS * COMPS):
                    both = pltpu.matmul_pop(totals[pair * COMPS * COMPS + ab])
                    summed = both[:, :LAGS] + both[:, LAGS:]
                    for half in range(2):
                        k, other = members[2 * pair + half]
                        out_ref[peer(k, other), ab] = summed[half * TILE : (half + 1) * TILE].astype(jnp.bfloat16)

    pl.run_scoped(
        correlate,
        *[pltpu.ACC(i // (COMPS * COMPS) % UNITS)((2 * TILE, WIDE), jnp.float32) for i in range(GROUP // 2 * COMPS * COMPS)],
    )
    all_first.wait_send()
    all_third.wait_send()
    second_bytes(N_BLK - 1, my_z).wait_send()


def body(spectra, quality):
    out = pl.pallas_call(
        kernel,
        out_shape=pltpu.VMEM((N_BLK, COMPS * COMPS, TILE, LAGS), jnp.bfloat16),
        in_specs=[pl.BlockSpec(memory_space=pl.ANY)] * 3,
        out_specs=pl.BlockSpec(memory_space=pltpu.VMEM),
        scratch_shapes=[
            pltpu.VMEM((TILE, COMPS, 2, BINS), jnp.bfloat16),
            pltpu.VMEM((COMPS, TILE), jnp.int32),
            pltpu.VMEM((DEPTH + LANES, 2 * LAGS), jnp.bfloat16),
            pltpu.VMEM((N_BAND, 2 * TILE, LANES), jnp.bfloat16),
            pltpu.VMEM((N_BAND, 1, 2 * LANES), jnp.float32),
            pltpu.VMEM((N_BAND, 1, 2 * LANES), jnp.float32),
            pltpu.VMEM((COMPS, CHUNKS, TILE, LANES), jnp.float32),
            pltpu.VMEM((COMPS, CHUNKS, TILE, LANES), jnp.float32),
            pltpu.VMEM((N_BLK, 16, LANES), jnp.bfloat16),
            pltpu.VMEM((GROUP, 2, 16, LANES), jnp.float32),
            pltpu.SemaphoreType.REGULAR,
            pltpu.SemaphoreType.DMA((3,)),
            pltpu.SemaphoreType.DMA,
            pltpu.SemaphoreType.DMA,
            pltpu.SemaphoreType.DMA,
            pltpu.SemaphoreType.DMA((RING,)),
            pltpu.SemaphoreType.DMA,
            pltpu.SemaphoreType.DMA,
        ],
        compiler_params=pltpu.CompilerParams(collective_id=0, has_side_effects=True),
    )(spectra, quality.T, jnp.asarray(lag_table()))
    return out.transpose(0, 2, 1, 3)[:, :, None]


def solution(mesh):
    placed = (P("blk", None, None, "band"), P("blk", None))
    return jax.shard_map(
        body,
        mesh=mesh,
        in_specs=placed,
        out_specs=P(None, "blk", "band", None, None),
        check_vma=False,
    )
```

```python
import math

import jax
import jax.numpy as jnp
import numpy as np
from jax import lax
from jax.experimental import pallas as pl
from jax.experimental.pallas import tpu as pltpu
from jax.sharding import PartitionSpec as P

F = 320
FIRST = 15
NFFT = 1500
MAXLAG = 64
LAGS = 128
COMPS = 3
TILE = 8
N_BLK = 32
N_BAND = 8
BINS = F // N_BAND
HALF = 64
CHUNKS = F // HALF
DEPTH = 2 * F
LANES = 128
RING = 8
GROUP = 8
WIDE = 2 * LANES
STEPS = 3
UNITS = 2
MESH = pl.DeviceIdType.MESH


def lag_table():
    bins = np.arange(F) + FIRST
    steps = 2 * np.arange(LAGS) - 2 * MAXLAG + 1
    index = bins[:, None] * steps[None, :] % (2 * NFFT)
    phase = (np.float32(math.pi / NFFT) * index.astype(np.float32)).astype(np.float64)
    factor = 1.0 / math.sqrt(F)
    both = np.stack([np.cos(phase) * factor, np.sin(phase) * factor])
    both = both.reshape(2, CHUNKS, HALF, LAGS).transpose(1, 0, 2, 3).reshape(DEPTH, LAGS)
    high = both.astype(jnp.bfloat16)
    low = (both - high.astype(np.float64)).astype(jnp.bfloat16)
    wide = np.concatenate([high, low], axis=1)
    return np.concatenate([wide, wide[-LANES:]], axis=0)


RING_ORDER = (0, 1, 2, 3, 7, 6, 5, 4)
HUB_Z = (3, 5, 6, 6, 6, 7, 7, 7)
HUB_ORDER = [4 * z + other for z in (4, 3, 5, 2, 6, 1, 7, 0) for other in range(4)]


def index_at(place):
    return ((place // 2) % 2 * RING + place // 4) * 2 + place % 2


def segments():
    found = []
    for p in range(N_BAND):
        at = 0
        while at < BINS:
            chunk, lane = divmod(p * BINS + at, HALF)
            length = min(BINS - at, HALF - lane)
            found.append((p, at, length, chunk, lane))
            at += length
    return found


def kernel(
    spec_hbm, qual_hbm, table_hbm, out_ref,
    spec_v, qual_v, table_v, pieces, rows_out, rows_in, left_same, left_cross, stations, wide_rows,
    all_in, load_sem, first_send, first_recv, second_send, second_recv, third_send, third_recv,
):
    me = lax.axis_index("blk")
    band = lax.axis_index("band")
    my_y = lax.div(me, 2 * RING)
    my_z = lax.rem(lax.div(me, 2), RING)
    my_core = lax.rem(me, 2)
    my_place = my_z * 4 + my_y * 2 + my_core

    def peer(k, other):
        flip_y, flip_core = divmod(other, 2)
        y = lax.rem(my_y + flip_y, 2)
        z = lax.rem(my_z + RING_ORDER[k], RING)
        core = lax.rem(my_core + flip_core, 2)
        return (y * RING + z) * 2 + core

    loads = [
        pltpu.make_async_copy(spec_hbm, spec_v, load_sem.at[0]),
        pltpu.make_async_copy(qual_hbm, qual_v, load_sem.at[1]),
        pltpu.make_async_copy(table_hbm, table_v, load_sem.at[2]),
    ]
    for load in loads:
        load.start()

    hub_z = HUB_Z[-1]
    for b in range(N_BAND - 1):
        hub_z = jnp.where(band == b, HUB_Z[b], hub_z)
    hub = 4 * hub_z + 2
    barrier = pltpu.get_barrier_semaphore()

    @pl.when(my_place != hub)
    def _():
        pl.semaphore_signal(barrier, inc=1, device_id=(index_at(hub), band), device_id_type=MESH)

    for step in range(1, N_BAND):
        pl.semaphore_signal(barrier, inc=1, device_id=(me, lax.rem(band + step, N_BAND)), device_id_type=MESH)

    loads[0].wait()
    loads[1].wait()

    quality = qual_v[...].astype(jnp.float32)
    row = lax.broadcasted_iota(jnp.int32, (TILE, TILE), 0)
    col = lax.broadcasted_iota(jnp.int32, (TILE, TILE), 1)
    raw = spec_v[...].astype(jnp.float32)
    parts = []
    for c in range(2):
        masked = []
        for a in range(COMPS):
            usable = jnp.sum(jnp.where(row == col, quality[a : a + 1, :], 0.0), axis=1, keepdims=True)
            masked.append(raw[:, a, c, :] * usable)
        masked.append(jnp.zeros((TILE, LANES - COMPS * BINS), jnp.float32))
        parts.append(jnp.concatenate(masked, axis=1))
    pieces[band] = jnp.concatenate(parts, axis=0).astype(jnp.bfloat16)
    flat = jnp.concatenate(parts, axis=1)
    for station in range(TILE):
        rows_out[station] = flat[station : station + 1, :]
    rows_in[band] = rows_out[band]

    pl.semaphore_wait(barrier, jnp.where(my_place == hub, N_BAND + N_BLK - 2, N_BAND - 1))

    @pl.when(my_place == hub)
    def _():
        for place in HUB_ORDER:
            @pl.when(my_place != place)
            def _():
                pl.semaphore_signal(all_in, inc=1, device_id=(index_at(place), band), device_id_type=MESH)

    def first(step):
        to = lax.rem(band + step, N_BAND)
        return pltpu.make_async_remote_copy(
            src_ref=rows_out.at[to], dst_ref=rows_in.at[band],
            send_sem=first_send, recv_sem=first_recv,
            device_id=(me, to), device_id_type=MESH,
        )

    def third(step):
        to = lax.rem(band + step, N_BAND)
        return pltpu.make_async_remote_copy(
            src_ref=pieces.at[band], dst_ref=pieces.at[band],
            send_sem=third_send, recv_sem=third_recv,
            device_id=(me, to), device_id_type=MESH,
        )

    def whole_bytes(ref, send_sem, recv_sem):
        return pltpu.make_async_remote_copy(
            src_ref=ref.at[pl.ds(0, N_BAND - 1)], dst_ref=ref.at[pl.ds(0, N_BAND - 1)],
            send_sem=send_sem, recv_sem=recv_sem,
            device_id=(me, lax.rem(band + 1, N_BAND)), device_id_type=MESH,
        )

    for step in (6, 2, 5, 7, 3, 1, 4):
        first(step).start()
    for step in (6, 2, 5, 7, 3, 1, 4):
        third(step).start()
    all_first = whole_bytes(rows_in, first_send, first_recv)
    all_third = whole_bytes(pieces, third_send, third_recv)

    lane = lax.broadcasted_iota(jnp.int32, (TILE, LANES), 1)

    def assemble(piece):
        whole = [[None] * CHUNKS for _ in range(COMPS)]
        for p, at, length, chunk, start in segments():
            for c in range(2):
                values = piece(p, c)
                for a in range(COMPS):
                    target = HALF * c + start
                    moved = pltpu.roll(values, (target - BINS * a - at) % LANES, 1)
                    if whole[a][chunk] is None:
                        whole[a][chunk] = moved
                    else:
                        here = (lane >= target) & (lane < target + length)
                        whole[a][chunk] = jnp.where(here, moved, whole[a][chunk])
        return whole

    all_first.wait_recv()
    mine = assemble(lambda p, c: jnp.broadcast_to(rows_in[p, :, c * LANES : (c + 1) * LANES], (TILE, LANES)))
    sublane = lax.broadcasted_iota(jnp.int32, (TILE, LANES), 0)
    halves = []
    for half in range(2):
        rows = jnp.zeros((TILE, LANES), jnp.float32)
        for r in range(TILE):
            if half * TILE + r < COMPS * CHUNKS:
                a, chunk = divmod(half * TILE + r, CHUNKS)
                rows = jnp.where(sublane == r, mine[a][chunk], rows)
        halves.append(rows)
    stations[me] = jnp.concatenate(halves, axis=0).astype(jnp.bfloat16)

    def second(to):
        return pltpu.make_async_remote_copy(
            src_ref=stations.at[me], dst_ref=stations.at[me],
            send_sem=second_send, recv_sem=second_recv.at[my_z],
            device_id=(to, band), device_id_type=MESH,
        )

    def second_bytes(count, z):
        return pltpu.make_async_remote_copy(
            src_ref=stations.at[pl.ds(0, count)], dst_ref=stations.at[pl.ds(0, count)],
            send_sem=second_send, recv_sem=second_recv.at[z],
            device_id=(lax.rem(me + 1, N_BLK), band), device_id_type=MESH,
        )

    @pl.when(my_place != hub)
    def _():
        pl.semaphore_wait(all_in, 1)

    for place in [4 * z + other for z in range(RING) for other in (1, 3, 0, 2)]:
        @pl.when(my_place != place)
        def _():
            second(index_at(place)).start()

    all_third.wait_recv()
    whole = assemble(lambda p, c: pieces[p, c * TILE : (c + 1) * TILE, :].astype(jnp.float32))

    for a in range(COMPS):
        for chunk in range(CHUNKS):
            here = whole[a][chunk]
            turned = pltpu.roll(here, HALF, 1)
            left_same[a, chunk] = jnp.where(lane < HALF, here, turned)
            left_cross[a, chunk] = jnp.where(lane < HALF, turned, -here)
    loads[2].wait()

    def split_cross(pair, a, b, chunk):
        rows = []
        at = b * CHUNKS + chunk
        for s in (2 * pair, 2 * pair + 1):
            straight = jnp.broadcast_to(wide_rows[s, 0, at : at + 1, :], (TILE, LANES))
            turned = jnp.broadcast_to(wide_rows[s, 1, at : at + 1, :], (TILE, LANES))
            rows.append(left_same[a, chunk] * straight + left_cross[a, chunk] * turned)
        value = jnp.concatenate(rows, axis=0)
        high = value.astype(jnp.bfloat16)
        return high, (value - high.astype(jnp.float32)).astype(jnp.bfloat16)

    def correlate(*totals):
        for group in range(N_BLK // GROUP):
            members = [divmod(group * GROUP + s, 4) for s in range(GROUP)]
            for k in sorted({k for k, _ in members}):
                second_bytes(4 if k else 3, lax.rem(my_z + RING_ORDER[k], RING)).wait_recv()
            for s, (k, other) in enumerate(members):
                arrived = stations[peer(k, other)].astype(jnp.float32)
                wide_rows[s, 0] = arrived
                wide_rows[s, 1] = pltpu.roll(arrived, HALF, 1)
            for step in range(STEPS):
                register = (group * STEPS + step) % 2
                weights = table_v[pl.ds(step * WIDE, WIDE), :]
                for unit in range(UNITS):
                    pltpu.matmul_push_rhs(weights, staging_register=register, mxu_index=unit)
                fresh = [True] * UNITS
                for pair in range(GROUP // 2):
                    unit = pair % UNITS
                    for b in range(COMPS):
                        for a in range(COMPS):
                            parts = [split_cross(pair, a, b, chunk) for chunk in range(2 * step, min(2 * step + 2, CHUNKS))]
                            sums = totals[pair * COMPS * COMPS + a * COMPS + b]
                            if len(parts) == 1:
                                operands = [jnp.concatenate(parts[0], axis=1)]
                            else:
                                operands = [jnp.concatenate([part[i] for part in parts], axis=1) for i in range(2)]
                            for operand in operands:
                                pltpu.matmul_acc_lhs(sums, operand, load_staged_rhs=register if fresh[unit] else None)
                                fresh[unit] = False
            for pair in range(GROUP // 2):
                for ab in range(COMPS * COMPS):
                    both = pltpu.matmul_pop(totals[pair * COMPS * COMPS + ab])
                    summed = both[:, :LAGS] + both[:, LAGS:]
                    for half in range(2):
                        k, other = members[2 * pair + half]
                        out_ref[peer(k, other), ab] = summed[half * TILE : (half + 1) * TILE].astype(jnp.bfloat16)

    pl.run_scoped(
        correlate,
        *[pltpu.ACC(i // (COMPS * COMPS) % UNITS)((2 * TILE, WIDE), jnp.float32) for i in range(GROUP // 2 * COMPS * COMPS)],
    )
    all_first.wait_send()
    all_third.wait_send()
    second_bytes(N_BLK - 1, my_z).wait_send()


def body(spectra, quality):
    out = pl.pallas_call(
        kernel,
        out_shape=pltpu.VMEM((N_BLK, COMPS * COMPS, TILE, LAGS), jnp.bfloat16),
        in_specs=[pl.BlockSpec(memory_space=pl.ANY)] * 3,
        out_specs=pl.BlockSpec(memory_space=pltpu.VMEM),
        scratch_shapes=[
            pltpu.VMEM((TILE, COMPS, 2, BINS), jnp.bfloat16),
            pltpu.VMEM((COMPS, TILE), jnp.int32),
            pltpu.VMEM((DEPTH + LANES, 2 * LAGS), jnp.bfloat16),
            pltpu.VMEM((N_BAND, 2 * TILE, LANES), jnp.bfloat16),
            pltpu.VMEM((N_BAND, 1, 2 * LANES), jnp.float32),
            pltpu.VMEM((N_BAND, 1, 2 * LANES), jnp.float32),
            pltpu.VMEM((COMPS, CHUNKS, TILE, LANES), jnp.float32),
            pltpu.VMEM((COMPS, CHUNKS, TILE, LANES), jnp.float32),
            pltpu.VMEM((N_BLK, 16, LANES), jnp.bfloat16),
            pltpu.VMEM((GROUP, 2, 16, LANES), jnp.float32),
            pltpu.SemaphoreType.REGULAR,
            pltpu.SemaphoreType.DMA((3,)),
            pltpu.SemaphoreType.DMA,
            pltpu.SemaphoreType.DMA,
            pltpu.SemaphoreType.DMA,
            pltpu.SemaphoreType.DMA((RING,)),
            pltpu.SemaphoreType.DMA,
            pltpu.SemaphoreType.DMA,
        ],
        compiler_params=pltpu.CompilerParams(collective_id=0, has_side_effects=True),
    )(spectra, quality.T, jnp.asarray(lag_table()))
    return out.transpose(0, 2, 1, 3)[:, :, None]


def solution(mesh):
    placed = (P("blk", None, None, "band"), P("blk", None))
    return jax.shard_map(
        body,
        mesh=mesh,
        in_specs=placed,
        out_specs=P(None, "blk", "band", None, None),
        check_vma=False,
    )
```
